256 devices in a mesh: gx: 16 (over y, z_lo, core), gy: 4 (over x), gz: 4 (over z_hi).
Axes of the slice: x: 4, y: 4, z: 8 (z_hi: 4, z_lo: 2; z = z_hi * 2 + z_lo), core: 2. Of those that a mesh axis runs over, the one named last changes fastest.
Arguments:
- features: bfloat16 [32, 64, 16, 1024], P(None, 'gx', 'gy', 'gz'), may hold values from -6 to 6
- conv_one: bfloat16 [32, 864], replicated, may hold values from -0.3125 to 0.3125
- conv_two: bfloat16 [32, 864], replicated, may hold values from -0.3125 to 0.3125
- conv_three: bfloat16 [64, 864], replicated, may hold values from -0.3125 to 0.3125
- conv_four: bfloat16 [64, 1728], replicated, may hold values from -0.21875 to 0.21875
- depth_one: bfloat16 [64, 27], replicated, may hold values from -1.25 to 1.25
- point_one: bfloat16 [128, 64], replicated, may hold values from -1 to 1
- depth_two: bfloat16 [128, 27], replicated, may hold values from -1.25 to 1.25
- point_two: bfloat16 [128, 128], replicated, may hold values from -0.75 to 0.75
- conv_five: bfloat16 [64, 5184], replicated, may hold values from -0.125 to 0.125
- conv_six: bfloat16 [32, 2592], replicated, may hold values from -0.125 to 0.125
Outputs:
- decoded: bfloat16 [32, 64, 16, 1024], P(None, 'gx', 'gy', 'gz')
The draws below stay inside these ranges and needn't reach their ends.
All inputs are finite; a program needn't handle non-finite values.
Results may differ from the reference program's by a relative error of at most 0.015.
Values may be sent and summed in bfloat16 or wider, within the bound.
No kernel may reach another device: no remote copies, remote signals or barrier semaphores. Data moves between devices by JAX's collectives and lax.ppermute only.
A program may use at most 64 MiB of HBM per device.

```python
import jax
import jax.numpy as jnp
from jax import lax

C1 = 32
C2 = 64
C3 = 128
NX = 64
NY = 16
NZ = 1024


def shard_levels(own_key, dims, cuts, smallest, largest):
    loudness = 1.0
    for axis_at, parts in cuts:
        draws = jax.random.uniform(jax.random.fold_in(jax.random.fold_in(own_key, 6), axis_at), (parts,), jnp.float32, smallest / len(cuts), largest / len(cuts))
        loudness = loudness * jnp.repeat(jnp.exp(draws), dims[axis_at] // parts).reshape((-1,) + (1,) * (len(dims) - 1 - axis_at))
    return loudness


def scatter_about(key, shape, width, limit, split=(), dtype=jnp.bfloat16):
    gain = shard_levels(key, shape, split, -0.22, 0.18) if split else 1.0
    entries = jax.random.normal(key, shape, jnp.float32) * width * gain
    return jnp.minimum(jnp.maximum(entries, -limit), limit).astype(dtype)


def setup_inputs(seed: int = 0) -> dict:
    arg_keys = jax.random.split(jax.random.key(seed), 12)
    return {
        "features": scatter_about(arg_keys[0], (C1, NX, NY, NZ), 1.0, 6.0, ((1, 16), (2, 4), (3, 4))),
        "conv_one": scatter_about(arg_keys[1], (C1, 27 * C1), (27 * C1 // 2) ** -0.5, 0.3125),
        "conv_two": scatter_about(arg_keys[2], (C1, 27 * C1), (27 * C1 // 2) ** -0.5, 0.3125),
        "conv_three": scatter_about(arg_keys[3], (C2, 27 * C1), (27 * C1 // 2) ** -0.5, 0.3125),
        "conv_four": scatter_about(arg_keys[4], (C2, 27 * C2), (27 * C2 // 2) ** -0.5, 0.21875),
        "depth_one": scatter_about(arg_keys[5], (C2, 27), 27 ** -0.5, 1.25),
        "point_one": scatter_about(arg_keys[6], (C3, C2), (C2 // 2) ** -0.5, 1.0),
        "depth_two": scatter_about(arg_keys[7], (C3, 27), 27 ** -0.5, 1.25),
        "point_two": scatter_about(arg_keys[8], (C3, C3), (C3 // 2) ** -0.5, 0.75),
        "conv_five": scatter_about(arg_keys[9], (C2, 27 * (C3 + C2)), (27 * (C3 + C2) // 2) ** -0.5, 0.125),
        "conv_six": scatter_about(arg_keys[10], (C1, 27 * (C2 + C1)), (27 * (C2 + C1)) ** -0.5, 0.125),
    }


def rectify(values):
    return jnp.maximum(values, 0.0)


def convolve(values, weight):
    channels = values.shape[0]
    width_out = weight.shape[0]
    kernel = weight.astype(jnp.float32).reshape(width_out, 3, 3, 3, channels).transpose(0, 4, 1, 2, 3)
    result = lax.conv_general_dilated(values.astype(jnp.float32)[None], kernel, (1, 1, 1), ((1, 1), (1, 1), (1, 1)), dimension_numbers=("NCDHW", "OIDHW", "NCDHW"), precision=lax.Precision.HIGHEST)
    return result[0]


def depthwise(values, tap_weights):
    channels = values.shape[0]
    kernel = tap_weights.astype(jnp.float32).reshape(channels, 1, 3, 3, 3)
    result = lax.conv_general_dilated(values.astype(jnp.float32)[None], kernel, (1, 1, 1), ((1, 1), (1, 1), (1, 1)), dimension_numbers=("NCDHW", "OIDHW", "NCDHW"), feature_group_count=channels, precision=lax.Precision.HIGHEST)
    return result[0]


def shrink(values):
    channels, size_x, size_y, size_z = values.shape
    return values.reshape(channels, size_x // 2, 2, size_y // 2, 2, size_z // 2, 2).max(axis=(2, 4, 6))


def enlarge(values):
    channels, size_x, size_y, size_z = values.shape
    grown = jnp.broadcast_to(values[:, :, None, :, None, :, None], (channels, size_x, 2, size_y, 2, size_z, 2))
    return grown.reshape(channels, 2 * size_x, 2 * size_y, 2 * size_z)


def pointwise(values, mixing):
    channels, size_x, size_y, size_z = values.shape
    flattened = values.reshape(channels, size_x * size_y * size_z)
    mixed_out = rectify(jnp.dot(mixing, flattened, preferred_element_type=jnp.float32))
    return mixed_out.astype(jnp.bfloat16).reshape(mixing.shape[0], size_x, size_y, size_z)


def reference(features, conv_one, conv_two, conv_three, conv_four, depth_one, point_one, depth_two, point_two, conv_five, conv_six):
    first = rectify(convolve(features, conv_one)).astype(jnp.bfloat16)
    skip = rectify(convolve(first, conv_two)).astype(jnp.bfloat16)
    half_in = shrink(skip)
    half_mid = rectify(convolve(half_in, conv_three)).astype(jnp.bfloat16)
    half_skip = rectify(convolve(half_mid, conv_four)).astype(jnp.bfloat16)
    quarter = shrink(half_skip)
    spread_one = depthwise(quarter, depth_one).astype(jnp.bfloat16)
    mixed_one = pointwise(spread_one, point_one)
    spread_two = depthwise(mixed_one, depth_two).astype(jnp.bfloat16)
    mixed_two = pointwise(spread_two, point_two)
    joined = jnp.concatenate([enlarge(mixed_two), half_skip], axis=0)
    half_out = rectify(convolve(joined, conv_five)).astype(jnp.bfloat16)
    joined_fine = jnp.concatenate([enlarge(half_out), skip], axis=0)
    return convolve(joined_fine, conv_six).astype(jnp.bfloat16)
```

```python
import jax
import jax.numpy as jnp
from jax import lax
from jax.experimental import pallas as pl
from jax.experimental.pallas import tpu as pltpu
from jax.sharding import PartitionSpec as P

BF = jnp.bfloat16
F32 = jnp.float32
PLANE = ("gx", "gy")
EVERY = ("gx", "gy", "gz")
VMEM_LIMIT = 60 * 1024 * 1024


def device_at(q, r, k):
    return ((q * 4 + r // 4) * 4 + r % 4) * 4 + k


def neighbour_pairs(step_x, step_z):
    pairs = []
    for q in range(4):
        for s in range(64):
            to_q, to_s = q + step_x, s + step_z
            if 0 <= to_q < 4 and 0 <= to_s < 64:
                pairs.append((device_at(q, s % 16, s // 16), device_at(to_q, to_s % 16, to_s // 16)))
    return pairs


GROUPS = [list(range(16 * q, 16 * q + 16)) for q in range(4)]
STEPS = [(-1, 0), (1, 0), (0, -1), (0, 1), (-1, -1), (-1, 1), (1, -1), (1, 1)]


def position():
    gx, gy, gz = lax.axis_index("gx"), lax.axis_index("gy"), lax.axis_index("gz")
    return gx // 4, gz * 16 + (gx % 4) * 4 + gy


def one_hot_order():
    row = lax.broadcasted_iota(jnp.int32, (512, 512), 0)
    lane = lax.broadcasted_iota(jnp.int32, (512, 512), 1)
    target = (row % 16) * 32 + row // 16
    return jnp.where(target == lane, 1.0, 0.0).astype(BF)


def to_rows_kernel(cells_ref, out_ref):
    turned = lax.dot_general(
        cells_ref[...], one_hot_order(), (((0,), (0,)), ((), ())), preferred_element_type=F32
    ).astype(BF)
    for slab in range(16):
        for x in range(4):
            out_ref[slab, x] = turned[16 * slab : 16 * slab + 16, 128 * x : 128 * x + 128]


def from_rows_kernel(rows_ref, out_ref):
    columns = [rows_ref[:, x].reshape(256, 128) for x in range(4)]
    turned = jnp.concatenate(columns, axis=1)
    out_ref[...] = lax.dot_general(
        one_hot_order(), turned, (((1,), (1,)), ((), ())), preferred_element_type=F32
    ).astype(BF)


def band(spread, out_ref, stride, first, used, lanes_in, lanes_out, grown):
    out_pos = lax.broadcasted_iota(jnp.int32, (used, 256), 1) // lanes_out
    base = 128 // lanes_in
    for dx in range(3):
        for dz in range(3):
            parts = []
            for dy in range(3):
                start = ((dx * 3 + dy) * 3 + dz) * stride + first
                parts.append(spread[start : start + used, :])
            for at in range(512 // lanes_in):
                rel = at - base
                if grown:
                    gap = out_pos - 2 * rel
                    block = jnp.where(
                        gap == -1,
                        parts[2],
                        jnp.where(
                            gap == 0,
                            parts[1] + parts[2],
                            jnp.where(
                                gap == 1, parts[0] + parts[1], jnp.where(gap == 2, parts[0], 0.0)
                            ),
                        ),
                    )
                    live = -1 <= rel and 2 * rel <= 256 // lanes_out
                else:
                    gap = rel - out_pos
                    block = jnp.where(
                        gap == -1,
                        parts[0],
                        jnp.where(gap == 0, parts[1], jnp.where(gap == 1, parts[2], 0.0)),
                    )
                    live = -1 <= rel <= 256 // lanes_out
                tap = dx * 3 + dz
                if not live:
                    block = jnp.zeros_like(block)
                out_ref[tap, at * lanes_in : at * lanes_in + used, :] = block.astype(BF)
                if used < lanes_in:
                    out_ref[tap, at * lanes_in + used : (at + 1) * lanes_in, :] = jnp.zeros(
                        (lanes_in - used, 256), BF
                    )


def spread_lanes(weight, lanes_out):
    outs = weight.shape[0]
    row = lax.broadcasted_iota(jnp.int32, (outs, 256), 0)
    lane = lax.broadcasted_iota(jnp.int32, (outs, 256), 1)
    chosen = jnp.where(lane % lanes_out == row, 1.0, 0.0).astype(BF)
    return lax.dot_general(weight, chosen, (((0,), (0,)), ((), ())), preferred_element_type=F32)


def encoder_weights_kernel(w1, w2, w3, w4, o1, o2, o3, o4):
    band(spread_lanes(w1[...], 32), o1, 32, 0, 32, 32, 32, False)
    band(spread_lanes(w2[...], 32), o2, 32, 0, 32, 32, 32, False)
    band(spread_lanes(w3[...], 64), o3, 32, 0, 32, 64, 64, False)
    band(spread_lanes(w4[...], 64), o4, 64, 0, 64, 64, 64, False)


def decoder_weights_kernel(w5, w6, o5u, o5s, o6u, o6s):
    wide = spread_lanes(w5[...], 64)
    band(wide, o5u, 192, 0, 128, 128, 64, True)
    band(wide, o5s, 192, 128, 64, 64, 64, False)
    fine = spread_lanes(w6[...], 32)
    band(fine, o6u, 96, 0, 64, 64, 32, True)
    band(fine, o6s, 96, 64, 32, 32, 32, False)


def convolve(fields, weights, acc_ref, planes, rows):
    taps = [(n, dx, dz) for n in range(len(fields)) for dx in range(3) for dz in range(3)]
    for g in range(2):
        total = None
        for at in range(0, len(taps), 2):
            chunk = taps[at : at + 2]
            left = [
                fields[n][dz, dx : dx + planes, :, 128 * g : 128 * g + 384].reshape(planes * rows, 384)
                for n, dx, dz in chunk
            ]
            right = [
                weights[n][dx * 3 + dz, 128 * (1 - g) : 128 * (1 - g) + 384, :] for n, dx, dz in chunk
            ]
            part = jnp.dot(
                jnp.concatenate(left, axis=1) if len(left) > 1 else left[0],
                jnp.concatenate(right, axis=0) if len(right) > 1 else right[0],
                preferred_element_type=F32,
            )
            total = part if total is None else total + part
        acc_ref[0:planes, 0:rows, 256 * g : 256 * g + 256] = total.reshape(planes, rows, 256)


def row_mask(rows, start, limit):
    at = lax.broadcasted_iota(jnp.int32, (rows, 512), 0) + start
    return (at >= 0) & (at < limit)


def store_turned(dest, plane, value, rows):
    dest[0, plane] = pltpu.roll(value, 1, 0).astype(BF)
    dest[1, plane] = value.astype(BF)
    dest[2, plane] = pltpu.roll(value, rows - 1, 0).astype(BF)


def encoder_kernel(
    own, xd, xu, zd, zu, dd, du, ud, uu, w1, w2, w3, w4,
    skip_out, half_out, field, turned, first, acc, half, mid, pooled,
):
    q, s = position()
    x0, z0 = 16 * q, 16 * s
    for i in range(4):
        for j in range(4):
            lanes = slice(128 * j, 128 * j + 128)
            field[8 + 4 * i : 12 + 4 * i, 8:24, lanes] = own[i, j].astype(F32)
            field[8 + 4 * i : 12 + 4 * i, 0:8, lanes] = zd[i, j].astype(F32)
            field[8 + 4 * i : 12 + 4 * i, 24:32, lanes] = zu[i, j].astype(F32)
    for i in range(2):
        for j in range(4):
            lanes = slice(128 * j, 128 * j + 128)
            low, high = slice(4 * i, 4 * i + 4), slice(24 + 4 * i, 28 + 4 * i)
            field[low, 8:24, lanes] = xd[i, j].astype(F32)
            field[high, 8:24, lanes] = xu[i, j].astype(F32)
            field[low, 0:8, lanes] = dd[i, j].astype(F32)
            field[low, 24:32, lanes] = du[i, j].astype(F32)
            field[high, 0:8, lanes] = ud[i, j].astype(F32)
            field[high, 24:32, lanes] = uu[i, j].astype(F32)

    @pl.loop(0, 28)
    def _(p):
        store_turned(turned, p, field[p + 2], 32)

    convolve([turned], [w1], acc, 26, 32)

    @pl.loop(0, 26)
    def _(p):
        x = x0 - 5 + p
        inside = row_mask(32, z0 - 8, 1024) & (x >= 0) & (x < 64)
        store_turned(first, p, jnp.where(inside, jnp.maximum(acc[p], 0.0), 0.0), 32)

    convolve([first], [w2], acc, 24, 32)

    @pl.loop(0, 12)
    def _(h):
        best = None
        for b in range(2):
            p = 2 * h + b
            x = x0 - 4 + p
            inside = row_mask(32, z0 - 8, 1024) & (x >= 0) & (x < 64)
            value = jnp.where(inside, jnp.maximum(acc[p], 0.0), 0.0)

            @pl.when((p >= 3) & (p < 21))
            def _():
                skip_out[0, p - 3] = pltpu.roll(value, 1, 0)[8:24].astype(BF)
                skip_out[1, p - 3] = value[8:24].astype(BF)
                skip_out[2, p - 3] = pltpu.roll(value, 31, 0)[8:24].astype(BF)

            best = value if best is None else jnp.maximum(best, value)
        best = jnp.maximum(best, pltpu.roll(best, 480, 1))
        for t in range(4):
            pooled[:, :] = best[:, 128 * t : 128 * t + 128]
            piece = jnp.maximum(pooled[pl.ds(0, 16, stride=2), :], pooled[pl.ds(1, 16, stride=2), :])
            half[0, h, :, 128 * t : 128 * t + 128] = pltpu.roll(piece, 1, 0).astype(BF)
            half[1, h, :, 128 * t : 128 * t + 128] = piece.astype(BF)
            half[2, h, :, 128 * t : 128 * t + 128] = pltpu.roll(piece, 15, 0).astype(BF)

    convolve([half], [w3], acc, 10, 16)

    @pl.loop(0, 10)
    def _(p):
        x = 8 * q - 1 + p
        inside = row_mask(16, 8 * s - 4, 512) & (x >= 0) & (x < 32)
        store_turned(mid, p, jnp.where(inside, jnp.maximum(acc[p, 0:16], 0.0), 0.0), 16)

    convolve([mid], [w4], acc, 8, 16)
    half_out[...] = jnp.maximum(acc[0:8, 4:12, :], 0.0).astype(BF)


def depthwise(source, taps, planes, offset):
    sums = []
    for t in range(4):
        total = jnp.zeros((planes, 8, 128), F32)
        for dx in range(3):
            for dy in range(3):
                at = t + dy - 1
                if not 0 <= at < 4:
                    continue
                for dz in range(3):
                    tap = (dx * 3 + dy) * 3 + dz
                    factor = taps[tap : tap + 1, :].reshape(1, 1, 128)
                    total += (
                        source[dx : dx + planes, pl.ds(offset + dz, 8), 128 * at : 128 * at + 128]
                        * factor
                    )
        sums.append(total.reshape(planes * 8, 128).astype(BF))
    return sums


def decoder_kernel(
    own, xd, xu, zd, zu, dd, du, ud, uu, skip, d1, p1, d2, p2, w5u, w5s, w6u, w6s,
    out, whole, sides, pooled, quarter, mixed, grown, ups, acc, tall, fine,
):
    q, s = position()
    blocks = [[dd, xd, du], [zd, own, zu], [ud, xu, uu]]
    for a in range(3):
        for b in range(3):
            whole[8 * a : 8 * a + 8, 8 * b : 8 * b + 8, :] = blocks[a][b][...].astype(F32)

    for p in range(12):
        for dz in range(3):
            sides[dz, p] = whole[p + 6, pl.ds(3 + dz, 16), :].astype(BF)

    quarter[...] = jnp.zeros_like(quarter)

    @pl.loop(0, 10)
    def _(p):
        best = jnp.maximum(whole[2 * p + 2], whole[2 * p + 3])
        best = jnp.maximum(best, pltpu.roll(best, 448, 1))
        for t in range(4):
            pooled[0:24, :] = best[:, 128 * t : 128 * t + 128]
            quarter[p, 0:12, 128 * t : 128 * t + 128] = jnp.maximum(
                pooled[pl.ds(0, 12, stride=2), :], pooled[pl.ds(1, 12, stride=2), :]
            )

    mixed[...] = jnp.zeros_like(mixed)
    spread = depthwise(quarter, d1, 8, 1)
    plane = lax.broadcasted_iota(jnp.int32, (8, 8, 128), 0) + (4 * q - 2)
    row = lax.broadcasted_iota(jnp.int32, (8, 8, 128), 1) + (4 * s - 2)
    inside = (plane >= 0) & (plane < 16) & (row >= 0) & (row < 256)
    for t in range(4):
        value = lax.dot_general(
            spread[t], p1[...], (((1,), (1,)), ((), ())), preferred_element_type=F32
        ).reshape(8, 8, 128)
        value = jnp.where(inside, jnp.maximum(value, 0.0), 0.0)
        mixed[:, 0:8, 128 * t : 128 * t + 128] = value.astype(BF).astype(F32)

    spread = depthwise(mixed, d2, 6, 0)
    plane = lax.broadcasted_iota(jnp.int32, (6, 8, 128), 0) + (4 * q - 1)
    row = lax.broadcasted_iota(jnp.int32, (6, 8, 128), 1) + (4 * s - 1)
    inside = (plane >= 0) & (plane < 16) & (row >= 0) & (row < 256)
    grown[...] = jnp.zeros_like(grown)
    for t in range(4):
        value = lax.dot_general(
            spread[t], p2[...], (((1,), (1,)), ((), ())), preferred_element_type=F32
        ).reshape(6, 8, 128)
        value = jnp.where(inside, jnp.maximum(value, 0.0), 0.0)
        for p in range(6):
            grown[pl.ds(8, 8, stride=2), :] = value[p]
            grown[pl.ds(9, 8, stride=2), :] = value[p]
            for dz in range(3):
                rows = grown[pl.ds(5 + dz, 16), :].astype(BF)
                ups[dz, 2 * p, :, 128 * t : 128 * t + 128] = rows
                ups[dz, 2 * p + 1, :, 128 * t : 128 * t + 128] = rows

    convolve([ups, sides], [w5u, w5s], acc, 10, 16)

    @pl.loop(0, 10)
    def _(p):
        x = 8 * q - 1 + p
        inside = row_mask(16, 8 * s - 4, 512) & (x >= 0) & (x < 32)
        value = jnp.where(inside, jnp.maximum(acc[p], 0.0), 0.0)
        for t in range(4):
            tall[pl.ds(0, 16, stride=2), :] = value[:, 128 * t : 128 * t + 128]
            tall[pl.ds(1, 16, stride=2), :] = value[:, 128 * t : 128 * t + 128]
            for dz in range(3):
                rows = tall[pl.ds(7 + dz, 16), :].astype(BF)

                @pl.when(p > 0)
                def _():
                    fine[dz, 2 * p - 1, :, 128 * t : 128 * t + 128] = rows

                @pl.when(p < 9)
                def _():
                    fine[dz, 2 * p, :, 128 * t : 128 * t + 128] = rows

    convolve([fine, skip], [w6u, w6s], acc, 16, 16)
    for i in range(4):
        for j in range(4):
            out[i, j] = acc[4 * i : 4 * i + 4, :, 128 * j : 128 * j + 128].astype(BF)


def call(kernel, outs, scratch=(), flops=0):
    whole = pl.BlockSpec(memory_space=pltpu.VMEM)

    def run(*args):
        return pl.pallas_call(
            kernel,
            out_shape=outs,
            in_specs=[whole] * len(args),
            out_specs=jax.tree.map(lambda _: whole, outs),
            scratch_shapes=list(scratch),
            compiler_params=pltpu.CompilerParams(vmem_limit_bytes=VMEM_LIMIT),
            cost_estimate=pl.CostEstimate(flops=flops, bytes_accessed=4 << 20, transcendentals=0),
        )(*args)

    return run


def shape(*dims):
    return jax.ShapeDtypeStruct(dims, BF)


def local(
    features, conv_one, conv_two, conv_three, conv_four, depth_one, point_one, depth_two, point_two,
    conv_five, conv_six,
):
    taps_one = jnp.pad(depth_one.astype(F32).T, ((0, 5), (0, 64)))
    taps_two = jnp.pad(depth_two.astype(F32).T, ((0, 5), (0, 0)))
    mix_one = jnp.pad(point_one, ((0, 0), (0, 64)))
    bands = shape(9, 512, 256)

    rows = call(to_rows_kernel, shape(16, 4, 16, 128))(features.reshape(512, 256))
    own = lax.all_to_all(rows, PLANE, 0, 0, tiled=True, axis_index_groups=GROUPS)
    own = own.reshape(4, 4, 4, 16, 128)
    cut_x = {-1: slice(0, 2), 0: slice(0, 4), 1: slice(2, 4)}
    cut_z = {-1: slice(0, 8), 0: slice(0, 16), 1: slice(8, 16)}
    got = {}
    for a, b in STEPS:
        piece = own[cut_x[a], :, :, cut_z[b], :]
        got[(-a, -b)] = lax.ppermute(piece, EVERY, neighbour_pairs(a, b))
    w1, w2, w3, w4 = call(encoder_weights_kernel, (bands,) * 4)(
        conv_one, conv_two, conv_three, conv_four
    )
    skip, half_skip = call(
        encoder_kernel,
        (shape(3, 18, 16, 512), shape(8, 8, 512)),
        [
            pltpu.VMEM((32, 32, 512), F32),
            pltpu.VMEM((3, 28, 32, 512), BF),
            pltpu.VMEM((3, 26, 32, 512), BF),
            pltpu.VMEM((26, 32, 512), F32),
            pltpu.VMEM((3, 12, 16, 512), BF),
            pltpu.VMEM((3, 10, 16, 512), BF),
            pltpu.VMEM((32, 128), F32),
        ],
        flops=6 << 30,
    )(own, *[got[step] for step in STEPS], w1, w2, w3, w4)
    around = {}
    for a, b in STEPS:
        around[(-a, -b)] = lax.ppermute(half_skip, EVERY, neighbour_pairs(a, b))
    w5u, w5s, w6u, w6s = call(decoder_weights_kernel, (bands,) * 4)(conv_five, conv_six)
    rows = call(
        decoder_kernel,
        shape(4, 4, 4, 16, 128),
        [
            pltpu.VMEM((24, 24, 512), F32),
            pltpu.VMEM((3, 12, 16, 512), BF),
            pltpu.VMEM((32, 128), F32),
            pltpu.VMEM((10, 16, 512), F32),
            pltpu.VMEM((8, 16, 512), F32),
            pltpu.VMEM((32, 128), F32),
            pltpu.VMEM((3, 12, 16, 512), BF),
            pltpu.VMEM((16, 16, 512), F32),
            pltpu.VMEM((32, 128), F32),
            pltpu.VMEM((3, 18, 16, 512), BF),
        ],
        flops=2 << 30,
    )(
        half_skip, *[around[step] for step in STEPS], skip,
        taps_one, mix_one, taps_two, point_two, w5u, w5s, w6u, w6s,
    )
    back = lax.all_to_all(
        rows.reshape(16, 4, 16, 128), PLANE, 0, 0, tiled=True, axis_index_groups=GROUPS
    )
    return call(from_rows_kernel, shape(512, 256))(back).reshape(32, 4, 4, 256)


def solution(mesh):
    in_specs = (P(None, "gx", "gy", "gz"), P(), P(), P(), P(), P(), P(), P(), P(), P(), P())
    out_specs = P(None, "gx", "gy", "gz")
    return jax.shard_map(local, mesh=mesh, in_specs=in_specs, out_specs=out_specs, check_vma=False)
```

```python
import jax
import jax.numpy as jnp
from jax import lax
from jax.experimental import pallas as pl
from jax.experimental.pallas import tpu as pltpu
from jax.sharding import PartitionSpec as P

BF = jnp.bfloat16
F32 = jnp.float32
PLANE = ("gx", "gy")
EVERY = ("gx", "gy", "gz")
LIMITS = (24, 24, 32, 32)


def slab_at(z_low, across, core):
    step = across + z_low * (3 - 2 * across)
    return 8 * z_low + 2 * step + (core + step) % 2


SLABS = [slab_at(rank // 8, rank % 4, rank // 4 % 2) for rank in range(16)]


def device_at(q, slab, k):
    rank = SLABS.index(slab)
    return ((q * 4 + rank // 4) * 4 + rank % 4) * 4 + k


def swap_pairs(step_x, step_z, parity):
    pairs = []
    for q in range(4):
        for s in range(64):
            to_q, to_s = q + step_x, s + step_z
            if (q * step_x + s * step_z) % 2 == parity and to_q < 4 and to_s < 64:
                here = device_at(q, s % 16, s // 16)
                there = device_at(to_q, to_s % 16, to_s // 16)
                pairs += [(here, there), (there, here)]
    return pairs


GROUPS = [list(range(16 * q, 16 * q + 16)) for q in range(4)]


def position():
    gx, gy, gz = lax.axis_index("gx"), lax.axis_index("gy"), lax.axis_index("gz")
    return gx // 4, gz * 16 + slab_at(gx // 2 % 2, gy, gx % 2)


def one_hot_order():
    row = lax.broadcasted_iota(jnp.int32, (512, 512), 0)
    lane = lax.broadcasted_iota(jnp.int32, (512, 512), 1)
    target = (row % 16) * 32 + row // 16
    return jnp.where(target == lane, 1.0, 0.0).astype(BF)


def to_rows_kernel(cells_ref, out_ref):
    turned = lax.dot_general(
        cells_ref[...], one_hot_order(), (((0,), (0,)), ((), ())), preferred_element_type=F32
    ).astype(BF)
    for rank, slab in enumerate(SLABS):
        for x in range(4):
            out_ref[rank, x] = turned[16 * slab : 16 * slab + 16, 128 * x : 128 * x + 128]


def from_rows_kernel(rows_ref, out_ref):
    columns = [
        jnp.concatenate([rows_ref[SLABS.index(slab), x] for slab in range(16)], axis=0) for x in range(4)
    ]
    turned = jnp.concatenate(columns, axis=1)
    out_ref[...] = lax.dot_general(
        one_hot_order(), turned, (((1,), (1,)), ((), ())), preferred_element_type=F32
    ).astype(BF)


def band(spread, out_ref, stride, first, used, lanes_in, lanes_out, grown):
    per_tile = 128 // lanes_out
    base = 128 // lanes_in
    group = lax.broadcasted_iota(jnp.int32, (used, 128), 1) // lanes_out
    chosen = [jnp.where(group == j, 1.0, 0.0).astype(BF) for j in range(per_tile)]
    empty = jnp.zeros((lanes_in, 128), BF)
    for dx in range(3):
        for dz in range(3):
            tap = dx * 3 + dz
            parts = []
            for dy in range(3):
                start = ((dx * 3 + dy) * 3 + dz) * stride + first
                parts.append(spread[start : start + used, :])
            if grown:
                pieces = {-1: parts[2], 0: parts[1] + parts[2], 1: parts[0] + parts[1], 2: parts[0]}
            else:
                pieces = {1: parts[0], 0: parts[1], -1: parts[2]}
            pieces = {gap: piece.astype(BF) for gap, piece in pieces.items()}
            made = {}
            for at in range(512 // lanes_in):
                for tile in range(2):
                    key = (2 if grown else 1) * (at - base) - per_tile * tile
                    if key not in made:
                        block = None
                        for gap, piece in pieces.items():
                            if 0 <= key + gap < per_tile:
                                term = piece * chosen[key + gap]
                                block = term if block is None else block + term
                        made[key] = block
                    block = made[key]
                    lanes = slice(128 * tile, 128 * tile + 128)
                    if block is None:
                        out_ref[tap, at * lanes_in : (at + 1) * lanes_in, lanes] = empty
                    else:
                        out_ref[tap, at * lanes_in : at * lanes_in + used, lanes] = block
                        if used < lanes_in:
                            out_ref[tap, at * lanes_in + used : (at + 1) * lanes_in, lanes] = empty[
                                : lanes_in - used
                            ]


def spread_lanes(weight, lanes_out):
    outs = weight.shape[0]
    row = lax.broadcasted_iota(jnp.int32, (outs, 128), 0)
    lane = lax.broadcasted_iota(jnp.int32, (outs, 128), 1)
    chosen = jnp.where(lane % lanes_out == row, 1.0, 0.0).astype(BF)
    return lax.dot_general(weight, chosen, (((0,), (0,)), ((), ())), preferred_element_type=F32)


def encoder_weights_kernel(w1, w2, w3, w4, o1, o2, o3, o4):
    band(spread_lanes(w1[...], 32), o1, 32, 0, 32, 32, 32, False)
    band(spread_lanes(w2[...], 32), o2, 32, 0, 32, 32, 32, False)
    band(spread_lanes(w3[...], 64), o3, 32, 0, 32, 64, 64, False)
    band(spread_lanes(w4[...], 64), o4, 64, 0, 64, 64, 64, False)


def decoder_weights_kernel(w5, w6, o5u, o5s, o6u, o6s):
    wide = spread_lanes(w5[...], 64)
    band(wide, o5u, 192, 0, 128, 128, 64, True)
    band(wide, o5s, 192, 128, 64, 64, 64, False)
    fine = spread_lanes(w6[...], 32)
    band(fine, o6u, 96, 0, 64, 64, 32, True)
    band(fine, o6s, 96, 64, 32, 32, 32, False)


def convolve(fields, weights, acc_ref, planes, rows):
    taps = [(n, dx, dz) for n in range(len(fields)) for dx in range(3) for dz in range(3)]
    for g in range(2):
        total = None
        for at in range(0, len(taps), 2):
            chunk = taps[at : at + 2]
            left = [
                fields[n][dz, dx : dx + planes, :, 128 * g : 128 * g + 384].reshape(planes * rows, 384)
                for n, dx, dz in chunk
            ]
            right = [
                weights[n][dx * 3 + dz, 128 * (1 - g) : 128 * (1 - g) + 384, :] for n, dx, dz in chunk
            ]
            part = jnp.dot(
                jnp.concatenate(left, axis=1) if len(left) > 1 else left[0],
                jnp.concatenate(right, axis=0) if len(right) > 1 else right[0],
                preferred_element_type=F32,
            )
            total = part if total is None else total + part
        acc_ref[0:planes, 0:rows, 256 * g : 256 * g + 256] = total.reshape(planes, rows, 256)


def row_mask(rows, start, limit):
    at = lax.broadcasted_iota(jnp.int32, (rows, 512), 0) + start
    return (at >= 0) & (at < limit)


def store_turned(dest, plane, value, rows):
    dest[0, plane] = pltpu.roll(value, 1, 0).astype(BF)
    dest[1, plane] = value.astype(BF)
    dest[2, plane] = pltpu.roll(value, rows - 1, 0).astype(BF)


def encoder_kernel(
    own, x1, x2, z1, z2, w1, w2, w3, w4,
    skip_out, half_out, field, turned, first, acc, half, mid, pooled,
):
    q, s = position()
    x0, z0 = 16 * q, 16 * s
    plane_1 = 24 * (1 - q % 2)
    plane_2 = 24 - plane_1
    row_1 = pl.multiple_of(24 * (1 - s % 2), 8)
    row_2 = pl.multiple_of(24 * (s % 2), 8)
    starts = [plane_1, plane_1 + 4, 8, 12, 16, 20, plane_2, plane_2 + 4]
    for i in range(8):
        planes = pl.ds(starts[i], 4)
        source, at = (x1, i) if i < 2 else ((own, i - 2) if i < 6 else (x2, i - 6))
        for j in range(4):
            lanes = slice(128 * j, 128 * j + 128)
            field[planes, 8:24, lanes] = source[at, j].astype(F32)
            field[planes, pl.ds(row_1, 8), lanes] = z1[i, j].astype(F32)
            field[planes, pl.ds(row_2, 8), lanes] = z2[i, j].astype(F32)

    @pl.loop(0, 28)
    def _(p):
        store_turned(turned, p, field[p + 2], 32)

    convolve([turned], [w1], acc, 26, 32)

    @pl.loop(0, 26)
    def _(p):
        x = x0 - 5 + p
        inside = row_mask(32, z0 - 8, 1024) & (x >= 0) & (x < 64)
        store_turned(first, p, jnp.where(inside, jnp.maximum(acc[p], 0.0), 0.0), 32)

    convolve([first], [w2], acc, 24, 32)

    @pl.loop(0, 12)
    def _(h):
        best = None
        for b in range(2):
            p = 2 * h + b
            x = x0 - 4 + p
            inside = row_mask(32, z0 - 8, 1024) & (x >= 0) & (x < 64)
            value = jnp.where(inside, jnp.maximum(acc[p], 0.0), 0.0)

            @pl.when((p >= 3) & (p < 21))
            def _():
                skip_out[0, p - 3] = pltpu.roll(value, 1, 0)[8:24].astype(BF)
                skip_out[1, p - 3] = value[8:24].astype(BF)
                skip_out[2, p - 3] = pltpu.roll(value, 31, 0)[8:24].astype(BF)

            best = value if best is None else jnp.maximum(best, value)
        best = jnp.maximum(best, pltpu.roll(best, 480, 1))
        for t in range(4):
            pooled[:, :] = best[:, 128 * t : 128 * t + 128]
            piece = jnp.maximum(pooled[pl.ds(0, 16, stride=2), :], pooled[pl.ds(1, 16, stride=2), :])
            half[0, h, :, 128 * t : 128 * t + 128] = pltpu.roll(piece, 1, 0).astype(BF)
            half[1, h, :, 128 * t : 128 * t + 128] = piece.astype(BF)
            half[2, h, :, 128 * t : 128 * t + 128] = pltpu.roll(piece, 15, 0).astype(BF)

    convolve([half], [w3], acc, 10, 16)

    @pl.loop(0, 10)
    def _(p):
        x = 8 * q - 1 + p
        inside = row_mask(16, 8 * s - 4, 512) & (x >= 0) & (x < 32)
        store_turned(mid, p, jnp.where(inside, jnp.maximum(acc[p, 0:16], 0.0), 0.0), 16)

    convolve([mid], [w4], acc, 8, 16)
    half_out[...] = jnp.maximum(acc[0:8, 4:12, :], 0.0).astype(BF)


def depthwise(source, taps, planes, offset):
    sums = []
    for t in range(4):
        total = jnp.zeros((planes, 8, 128), F32)
        for dx in range(3):
            for dy in range(3):
                at = t + dy - 1
                if not 0 <= at < 4:
                    continue
                for dz in range(3):
                    tap = (dx * 3 + dy) * 3 + dz
                    factor = taps[tap : tap + 1, :].reshape(1, 1, 128)
                    total += (
                        source[dx : dx + planes, pl.ds(offset + dz, 8), 128 * at : 128 * at + 128]
                        * factor
                    )
        sums.append(total.reshape(planes * 8, 128).astype(BF))
    return sums


def decoder_kernel(
    own, x1, x2, z1, z2, skip, d1, p1, d2, p2, w5u, w5s, w6u, w6s,
    out, whole, sides, pooled, quarter, mixed, grown, ups, acc, tall, fine,
):
    q, s = position()
    plane_1 = 14 * (1 - q % 2)
    plane_2 = 14 - plane_1
    row_1 = pl.multiple_of(16 * (1 - s % 2), 8)
    row_2 = pl.multiple_of(16 * (s % 2), 8)
    for start, size, source, at in ((plane_1, 6, x1, 0), (6, 8, own, 6), (plane_2, 6, x2, 14)):
        whole[pl.ds(start, size), 8:16, :] = source[...].astype(F32)
        whole[pl.ds(start, size), pl.ds(row_1, 8), :] = z1[at : at + size].astype(F32)
        whole[pl.ds(start, size), pl.ds(row_2, 8), :] = z2[at : at + size].astype(F32)

    for p in range(12):
        for dz in range(3):
            sides[dz, p] = whole[p + 4, pl.ds(3 + dz, 16), :].astype(BF)

    quarter[...] = jnp.zeros_like(quarter)

    @pl.loop(0, 10)
    def _(p):
        best = jnp.maximum(whole[2 * p], whole[2 * p + 1])
        best = jnp.maximum(best, pltpu.roll(best, 448, 1))
        for t in range(4):
            pooled[0:24, :] = best[:, 128 * t : 128 * t + 128]
            quarter[p, 0:12, 128 * t : 128 * t + 128] = jnp.maximum(
                pooled[pl.ds(0, 12, stride=2), :], pooled[pl.ds(1, 12, stride=2), :]
            )

    mixed[...] = jnp.zeros_like(mixed)
    spread = depthwise(quarter, d1, 8, 1)
    plane = lax.broadcasted_iota(jnp.int32, (8, 8, 128), 0) + (4 * q - 2)
    row = lax.broadcasted_iota(jnp.int32, (8, 8, 128), 1) + (4 * s - 2)
    inside = (plane >= 0) & (plane < 16) & (row >= 0) & (row < 256)
    for t in range(4):
        value = lax.dot_general(
            spread[t], p1[...], (((1,), (1,)), ((), ())), preferred_element_type=F32
        ).reshape(8, 8, 128)
        value = jnp.where(inside, jnp.maximum(value, 0.0), 0.0)
        mixed[:, 0:8, 128 * t : 128 * t + 128] = value.astype(BF).astype(F32)

    spread = depthwise(mixed, d2, 6, 0)
    plane = lax.broadcasted_iota(jnp.int32, (6, 8, 128), 0) + (4 * q - 1)
    row = lax.broadcasted_iota(jnp.int32, (6, 8, 128), 1) + (4 * s - 1)
    inside = (plane >= 0) & (plane < 16) & (row >= 0) & (row < 256)
    grown[...] = jnp.zeros_like(grown)
    for t in range(4):
        value = lax.dot_general(
            spread[t], p2[...], (((1,), (1,)), ((), ())), preferred_element_type=F32
        ).reshape(6, 8, 128)
        value = jnp.where(inside, jnp.maximum(value, 0.0), 0.0)
        for p in range(6):
            grown[pl.ds(8, 8, stride=2), :] = value[p]
            grown[pl.ds(9, 8, stride=2), :] = value[p]
            for dz in range(3):
                rows = grown[pl.ds(5 + dz, 16), :].astype(BF)
                ups[dz, 2 * p, :, 128 * t : 128 * t + 128] = rows
                ups[dz, 2 * p + 1, :, 128 * t : 128 * t + 128] = rows

    convolve([ups, sides], [w5u, w5s], acc, 10, 16)

    @pl.loop(0, 10)
    def _(p):
        x = 8 * q - 1 + p
        inside = row_mask(16, 8 * s - 4, 512) & (x >= 0) & (x < 32)
        value = jnp.where(inside, jnp.maximum(acc[p], 0.0), 0.0)
        for t in range(4):
            tall[pl.ds(0, 16, stride=2), :] = value[:, 128 * t : 128 * t + 128]
            tall[pl.ds(1, 16, stride=2), :] = value[:, 128 * t : 128 * t + 128]
            for dz in range(3):
                rows = tall[pl.ds(7 + dz, 16), :].astype(BF)

                @pl.when(p > 0)
                def _():
                    fine[dz, 2 * p - 1, :, 128 * t : 128 * t + 128] = rows

                @pl.when(p < 9)
                def _():
                    fine[dz, 2 * p, :, 128 * t : 128 * t + 128] = rows

    convolve([fine, skip], [w6u, w6s], acc, 16, 16)
    for i in range(4):
        for j in range(4):
            out[i, j] = acc[4 * i : 4 * i + 4, :, 128 * j : 128 * j + 128].astype(BF)


def call(kernel, outs, scratch=(), flops=0, limit=8):
    whole = pl.BlockSpec(memory_space=pltpu.VMEM)

    def run(*args):
        return pl.pallas_call(
            kernel,
            out_shape=outs,
            in_specs=[whole] * len(args),
            out_specs=jax.tree.map(lambda _: whole, outs),
            scratch_shapes=list(scratch),
            compiler_params=pltpu.CompilerParams(vmem_limit_bytes=limit << 20),
            cost_estimate=pl.CostEstimate(flops=flops, bytes_accessed=4 << 20, transcendentals=0),
        )(*args)

    return run


def shape(*dims):
    return jax.ShapeDtypeStruct(dims, BF)


def local(
    features, conv_one, conv_two, conv_three, conv_four, depth_one, point_one, depth_two, point_two,
    conv_five, conv_six,
):
    taps_one = jnp.pad(depth_one.astype(F32).T, ((0, 5), (0, 64)))
    taps_two = jnp.pad(depth_two.astype(F32).T, ((0, 5), (0, 0)))
    mix_one = jnp.pad(point_one, ((0, 0), (0, 64)))
    bands = shape(9, 512, 256)

    rows = call(to_rows_kernel, shape(16, 4, 16, 128))(features.reshape(512, 256))
    own = lax.all_to_all(rows, PLANE, 0, 0, tiled=True, axis_index_groups=GROUPS)
    own = own.reshape(4, 4, 4, 16, 128)
    q, s = position()
    x_swaps = [swap_pairs(1, 0, parity) for parity in range(2)]
    z_swaps = [swap_pairs(0, 1, parity) for parity in range(2)]
    x_got = []
    for turn in range(2):
        start = jnp.where((q + turn) % 2 == 0, 2, 0)
        piece = lax.dynamic_slice_in_dim(own, start, 2, 0)
        x_got.append(lax.ppermute(piece, EVERY, x_swaps[turn]))
    broad = jnp.concatenate([x_got[0], own, x_got[1]], axis=0)
    z_got = []
    for turn in range(2):
        piece = jnp.where((s + turn) % 2 == 0, broad[..., 8:16, :], broad[..., 0:8, :])
        z_got.append(lax.ppermute(piece, EVERY, z_swaps[turn]))
    w1, w2, w3, w4 = call(encoder_weights_kernel, (bands,) * 4, limit=LIMITS[0])(
        conv_one, conv_two, conv_three, conv_four
    )
    skip, half_skip = call(
        encoder_kernel,
        (shape(3, 18, 16, 512), shape(8, 8, 512)),
        [
            pltpu.VMEM((32, 32, 512), F32),
            pltpu.VMEM((3, 28, 32, 512), BF),
            pltpu.VMEM((3, 26, 32, 512), BF),
            pltpu.VMEM((26, 32, 512), F32),
            pltpu.VMEM((3, 12, 16, 512), BF),
            pltpu.VMEM((3, 10, 16, 512), BF),
            pltpu.VMEM((32, 128), F32),
        ],
        flops=6 << 30,
        limit=LIMITS[2],
    )(own, *x_got, *z_got, w1, w2, w3, w4)
    x_got = []
    for turn in range(2):
        start = jnp.where((q + turn) % 2 == 0, 2, 0)
        piece = lax.dynamic_slice_in_dim(half_skip, start, 6, 0)
        x_got.append(lax.ppermute(piece, EVERY, x_swaps[turn]))
    broad = jnp.concatenate([x_got[0], half_skip, x_got[1]], axis=0)
    z_got = [lax.ppermute(broad, EVERY, z_swaps[turn]) for turn in range(2)]
    w5u, w5s, w6u, w6s = call(decoder_weights_kernel, (bands,) * 4, limit=LIMITS[1])(conv_five, conv_six)
    rows = call(
        decoder_kernel,
        shape(4, 4, 4, 16, 128),
        [
            pltpu.VMEM((20, 24, 512), F32),
            pltpu.VMEM((3, 12, 16, 512), BF),
            pltpu.VMEM((32, 128), F32),
            pltpu.VMEM((10, 16, 512), F32),
            pltpu.VMEM((8, 16, 512), F32),
            pltpu.VMEM((32, 128), F32),
            pltpu.VMEM((3, 12, 16, 512), BF),
            pltpu.VMEM((16, 16, 512), F32),
            pltpu.VMEM((32, 128), F32),
            pltpu.VMEM((3, 18, 16, 512), BF),
        ],
        flops=2 << 30,
        limit=LIMITS[3],
    )(
        half_skip, *x_got, *z_got, skip,
        taps_one, mix_one, taps_two, point_two, w5u, w5s, w6u, w6s,
    )
    back = lax.all_to_all(
        rows.reshape(16, 4, 16, 128), PLANE, 0, 0, tiled=True, axis_index_groups=GROUPS
    )
    return call(from_rows_kernel, shape(512, 256))(back).reshape(32, 4, 4, 256)


def solution(mesh):
    in_specs = (P(None, "gx", "gy", "gz"), P(), P(), P(), P(), P(), P(), P(), P(), P(), P())
    out_specs = P(None, "gx", "gy", "gz")
    return jax.shard_map(local, mesh=mesh, in_specs=in_specs, out_specs=out_specs, check_vma=False)
```

```python
import jax
import jax.numpy as jnp
from jax import lax
from jax.experimental import pallas as pl
from jax.experimental.pallas import tpu as pltpu
from jax.sharding import PartitionSpec as P

BF = jnp.bfloat16
F32 = jnp.float32
PLANE = ("gx", "gy")
EVERY = ("gx", "gy", "gz")
LIMITS = (24, 24, 32, 32)


def slab_at(z_low, across, core):
    step = across + z_low * (3 - 2 * across)
    return 8 * z_low + 2 * step + (core + step) % 2


SLABS = [slab_at(rank // 8, rank % 4, rank // 4 % 2) for rank in range(16)]


def device_at(q, slab, k):
    rank = SLABS.index(slab)
    return ((q * 4 + rank // 4) * 4 + rank % 4) * 4 + k


def swap_pairs(step_x, step_z, parity):
    pairs = []
    for q in range(4):
        for s in range(64):
            to_q, to_s = q + step_x, s + step_z
            if (q * step_x + s * step_z) % 2 == parity and to_q < 4 and to_s < 64:
                here = device_at(q, s % 16, s // 16)
                there = device_at(to_q, to_s % 16, to_s // 16)
                pairs += [(here, there), (there, here)]
    return pairs


GROUPS = [list(range(16 * q, 16 * q + 16)) for q in range(4)]


def position():
    gx, gy, gz = lax.axis_index("gx"), lax.axis_index("gy"), lax.axis_index("gz")
    return gx // 4, gz * 16 + slab_at(gx // 2 % 2, gy, gx % 2)


def one_hot_order():
    row = lax.broadcasted_iota(jnp.int32, (512, 512), 0)
    lane = lax.broadcasted_iota(jnp.int32, (512, 512), 1)
    target = (row % 16) * 32 + row // 16
    return jnp.where(target == lane, 1.0, 0.0).astype(BF)


def to_rows_kernel(cells_ref, out_ref):
    turned = lax.dot_general(
        cells_ref[...], one_hot_order(), (((0,), (0,)), ((), ())), preferred_element_type=F32
    ).astype(BF)
    for rank, slab in enumerate(SLABS):
        for x in range(4):
            out_ref[rank, x] = turned[16 * slab : 16 * slab + 16, 128 * x : 128 * x + 128]


def from_rows_kernel(rows_ref, out_ref):
    columns = [
        jnp.concatenate([rows_ref[SLABS.index(slab), x] for slab in range(16)], axis=0) for x in range(4)
    ]
    turned = jnp.concatenate(columns, axis=1)
    out_ref[...] = lax.dot_general(
        one_hot_order(), turned, (((1,), (1,)), ((), ())), preferred_element_type=F32
    ).astype(BF)


def band(spread, out_ref, stride, first, used, lanes_in, lanes_out, grown=False):
    per_tile = 128 // lanes_out
    lead = 128 // lanes_in
    group = lax.broadcasted_iota(jnp.int32, (used, 128), 1) // lanes_out
    chosen = [jnp.where(group == j, 1.0, 0.0).astype(BF) for j in range(per_tile)]
    empty = jnp.zeros((lanes_in, 128), BF)
    for dx in range(3):
        for dz in range(3):
            tap = dx * 3 + dz
            parts = []
            for dy in range(3):
                start = ((dx * 3 + dy) * 3 + dz) * stride + first
                parts.append(spread[start : start + used, :])
            if grown:
                pieces = {-1: parts[2], 0: parts[1] + parts[2], 1: parts[0] + parts[1], 2: parts[0]}
            else:
                pieces = {1: parts[0], 0: parts[1], -1: parts[2]}
            pieces = {gap: piece.astype(BF) for gap, piece in pieces.items()}
            made = {}
            for at in range(out_ref.shape[1] // lanes_in):
                for tile in range(2):
                    key = (2 if grown else 1) * (at - lead) - per_tile * tile
                    if key not in made:
                        block = None
                        for gap, piece in pieces.items():
                            if 0 <= key + gap < per_tile:
                                term = piece * chosen[key + gap]
                                block = term if block is None else block + term
                        made[key] = block
                    block = made[key]
                    lanes = slice(128 * tile, 128 * tile + 128)
                    if block is None:
                        out_ref[tap, at * lanes_in : (at + 1) * lanes_in, lanes] = empty
                    else:
                        out_ref[tap, at * lanes_in : at * lanes_in + used, lanes] = block
                        if used < lanes_in:
                            out_ref[tap, at * lanes_in + used : (at + 1) * lanes_in, lanes] = empty[
                                : lanes_in - used
                            ]


def spread_lanes(weight, lanes_out):
    outs = weight.shape[0]
    row = lax.broadcasted_iota(jnp.int32, (outs, 128), 0)
    lane = lax.broadcasted_iota(jnp.int32, (outs, 128), 1)
    chosen = jnp.where(lane % lanes_out == row, 1.0, 0.0).astype(BF)
    return lax.dot_general(weight, chosen, (((0,), (0,)), ((), ())), preferred_element_type=F32)


def encoder_weights_kernel(w1, w2, w3, w4, o1, o2, o3, o4):
    band(spread_lanes(w1[...], 32), o1, 32, 0, 32, 32, 32)
    band(spread_lanes(w2[...], 32), o2, 32, 0, 32, 32, 32)
    band(spread_lanes(w3[...], 64), o3, 32, 0, 32, 64, 64)
    band(spread_lanes(w4[...], 64), o4, 64, 0, 64, 64, 64)


def decoder_weights_kernel(w5, w6, o5u, o5s, o6u, o6s):
    wide = spread_lanes(w5[...], 64)
    band(wide, o5u, 192, 0, 128, 128, 64, grown=True)
    band(wide, o5s, 192, 128, 64, 64, 64)
    fine = spread_lanes(w6[...], 32)
    band(fine, o6u, 96, 0, 64, 64, 32, grown=True)
    band(fine, o6s, 96, 64, 32, 32, 32)


def convolve(terms, planes, rows, g):
    taps = [
        (field[dz, dx : dx + planes, :, 128 * g : 128 * g + 384].reshape(planes * rows, 384),
         weights[dx * 3 + dz, 128 * (1 - g) : 128 * (1 - g) + 384, :])
        for field, weights in terms
        for dx in range(3)
        for dz in range(3)
    ]
    total = None
    for at in range(0, len(taps), 2):
        left = [left for left, _ in taps[at : at + 2]]
        right = [right for _, right in taps[at : at + 2]]
        part = jnp.dot(
            jnp.concatenate(left, axis=1), jnp.concatenate(right, axis=0), preferred_element_type=F32
        )
        total = part if total is None else total + part
    return total.reshape(planes, rows, 256)


def row_mask(rows, start, limit):
    at = lax.broadcasted_iota(jnp.int32, (rows, 512), 0) + start
    return (at >= 0) & (at < limit)


def store_turned(dest, plane, value, keep=slice(None)):
    dest[0, plane] = pltpu.roll(value, 1, 0)[keep].astype(BF)
    dest[1, plane] = value[keep].astype(BF)
    dest[2, plane] = pltpu.roll(value, value.shape[0] - 1, 0)[keep].astype(BF)


def x_blocks(own, x1, x2, q):
    plane_1 = 24 * (1 - q % 2)
    plane_2 = 24 - plane_1
    starts = [plane_1, plane_1 + 4, 8, 12, 16, 20, plane_2, plane_2 + 4]
    sources = [(x1, 0), (x1, 1), (own, 0), (own, 1), (own, 2), (own, 3), (x2, 0), (x2, 1)]
    return [(pl.ds(start, 4), source, i) for start, (source, i) in zip(starts, sources)]


def own_rows_kernel(own, x1, x2, w1, out, field, turned, acc):
    q, _ = position()
    for planes, source, i in x_blocks(own, x1, x2, q):
        for j in range(4):
            field[planes, :, 128 * j : 128 * j + 128] = source[i, j].astype(F32)

    @pl.loop(0, 28, unroll=4)
    def _(p):
        store_turned(turned, p, field[p + 2])

    for g in range(2):
        acc[:, :, 256 * g : 256 * g + 256] = convolve([(turned, w1)], 26, 16, g)

    @pl.loop(0, 26, unroll=2)
    def _(p):
        x = 16 * q - 5 + p
        out[p] = jnp.where((x >= 0) & (x < 64), jnp.maximum(acc[p], 0.0), 0.0).astype(BF)


def encoder_kernel(
    own, x1, x2, z1, z2, own_first, w1, w2, w3, w4,
    skip_out, half_out, field, turned, full, first, acc, half, mid, pooled,
):
    q, s = position()
    x0, z0 = 16 * q, 16 * s
    row_1 = pl.multiple_of(24 * (1 - s % 2), 8)
    row_2 = pl.multiple_of(24 * (s % 2), 8)
    for at, (planes, source, i) in enumerate(x_blocks(own, x1, x2, q)):
        for j in range(4):
            lanes = slice(128 * j, 128 * j + 128)
            field[planes, 8:24, lanes] = source[i, j].astype(F32)
            field[planes, pl.ds(row_1, 8), lanes] = z1[at, j].astype(F32)
            field[planes, pl.ds(row_2, 8), lanes] = z2[at, j].astype(F32)

    @pl.loop(0, 28, unroll=4)
    def _(p):
        for dz in range(3):
            turned[dz, p] = jnp.concatenate(
                [field[p + 2, pl.ds(dz, 8), :], field[p + 2, pl.ds(22 + dz, 8), :]], axis=0
            ).astype(BF)

    for g in range(2):
        acc[0:26, 0:16, 256 * g : 256 * g + 256] = convolve([(turned, w1)], 26, 16, g)

    for slot in range(2):
        full[slot, 0:8] = jnp.zeros((8, 512), F32)
        full[slot, 24:32] = jnp.zeros((8, 512), F32)
    row = lax.broadcasted_iota(jnp.int32, (16, 512), 0)
    row = jnp.where(row < 8, row + (z0 - 7), row + (z0 + 7))
    row_inside = (row >= 0) & (row < 1024)

    @pl.loop(0, 26, unroll=2)
    def _(p):
        x = x0 - 5 + p
        value = jnp.where(row_inside & (x >= 0) & (x < 64), jnp.maximum(acc[p, 0:16], 0.0), 0.0)
        slot = p % 2
        full[slot, 8:24] = own_first[p].astype(F32)
        full[slot, 1:9] = value[0:8]
        full[slot, 23:31] = value[8:16]
        store_turned(first, p, full[slot])

    for g in range(2):
        acc[0:24, :, 256 * g : 256 * g + 256] = convolve([(first, w2)], 24, 32, g)

    @pl.loop(0, 12, unroll=4)
    def _(h):
        best = None
        for b in range(2):
            p = 2 * h + b
            x = x0 - 4 + p
            inside = row_mask(32, z0 - 8, 1024) & (x >= 0) & (x < 64)
            value = jnp.where(inside, jnp.maximum(acc[p], 0.0), 0.0)
            store_turned(skip_out, jnp.where((p >= 3) & (p < 21), p - 3, 18), value, slice(8, 24))
            best = value if best is None else jnp.maximum(best, value)
        best = jnp.maximum(best, pltpu.roll(best, 480, 1))
        pieces = []
        for t in range(4):
            pooled[h % 4, t] = best[:, 128 * t : 128 * t + 128]
            pieces.append(
                jnp.maximum(
                    pooled[h % 4, t, pl.ds(0, 16, stride=2), :], pooled[h % 4, t, pl.ds(1, 16, stride=2), :]
                )
            )
        store_turned(half, h, jnp.concatenate(pieces, axis=1))

    for g in range(2):
        acc[0:10, 0:16, 256 * g : 256 * g + 256] = convolve([(half, w3)], 10, 16, g)

    @pl.loop(0, 10, unroll=5)
    def _(p):
        x = 8 * q - 1 + p
        inside = row_mask(16, 8 * s - 4, 512) & (x >= 0) & (x < 32)
        store_turned(mid, p, jnp.where(inside, jnp.maximum(acc[p, 0:16], 0.0), 0.0))

    for g in range(2):
        acc[0:8, 0:16, 256 * g : 256 * g + 256] = convolve([(mid, w4)], 8, 16, g)
    half_out[...] = jnp.maximum(acc[0:8, 4:12, :], 0.0).astype(BF)


def skip_kernel(skip, w6s, out):
    for g in range(2):
        out[:, :, 256 * g : 256 * g + 256] = convolve([(skip.at[:, 0:18], w6s)], 16, 16, g)


def depthwise(source, taps, planes, offset):
    sums = []
    for t in range(4):
        total = jnp.zeros((planes, 8, 128), F32)
        for dx in range(3):
            for dy in range(3):
                at = t + dy - 1
                if not 0 <= at < 4:
                    continue
                for dz in range(3):
                    tap = (dx * 3 + dy) * 3 + dz
                    factor = taps[tap : tap + 1, :].reshape(1, 1, 128)
                    total += (
                        source[dx : dx + planes, pl.ds(offset + dz, 8), 128 * at : 128 * at + 128]
                        * factor
                    )
        sums.append(total.reshape(planes * 8, 128).astype(BF))
    return sums


def decoder_kernel(
    own, x1, x2, z1, z2, skip_part, d1, p1, d2, p2, w5u, w5s, w6u,
    out, whole, sides, pooled, quarter, mixed, grown, ups, acc, tall, fine,
):
    q, s = position()
    plane_1 = 14 * (1 - q % 2)
    plane_2 = 14 - plane_1
    row_1 = pl.multiple_of(16 * (1 - s % 2), 8)
    row_2 = pl.multiple_of(16 * (s % 2), 8)
    for start, size, source, at in ((plane_1, 6, x1, 0), (6, 8, own, 6), (plane_2, 6, x2, 14)):
        whole[pl.ds(start, size), 8:16, :] = source[...].astype(F32)
        whole[pl.ds(start, size), pl.ds(row_1, 8), :] = z1[at : at + size].astype(F32)
        whole[pl.ds(start, size), pl.ds(row_2, 8), :] = z2[at : at + size].astype(F32)

    @pl.loop(0, 12, unroll=4)
    def _(p):
        for dz in range(3):
            sides[dz, p] = whole[p + 4, pl.ds(3 + dz, 16), :].astype(BF)

    quarter[...] = jnp.zeros_like(quarter)

    @pl.loop(0, 10, unroll=5)
    def _(p):
        best = jnp.maximum(whole[2 * p], whole[2 * p + 1])
        best = jnp.maximum(best, pltpu.roll(best, 448, 1))
        for t in range(4):
            pooled[0:24, :] = best[:, 128 * t : 128 * t + 128]
            quarter[p, 0:12, 128 * t : 128 * t + 128] = jnp.maximum(
                pooled[pl.ds(0, 12, stride=2), :], pooled[pl.ds(1, 12, stride=2), :]
            )

    mixed[...] = jnp.zeros_like(mixed)
    spread = depthwise(quarter, d1, 8, 1)
    plane = lax.broadcasted_iota(jnp.int32, (8, 8, 128), 0) + (4 * q - 2)
    row = lax.broadcasted_iota(jnp.int32, (8, 8, 128), 1) + (4 * s - 2)
    inside = (plane >= 0) & (plane < 16) & (row >= 0) & (row < 256)
    for t in range(4):
        value = lax.dot_general(
            spread[t], p1[...], (((1,), (1,)), ((), ())), preferred_element_type=F32
        ).reshape(8, 8, 128)
        value = jnp.where(inside, jnp.maximum(value, 0.0), 0.0)
        mixed[:, 0:8, 128 * t : 128 * t + 128] = value.astype(BF).astype(F32)

    spread = depthwise(mixed, d2, 6, 0)
    plane = lax.broadcasted_iota(jnp.int32, (6, 8, 128), 0) + (4 * q - 1)
    row = lax.broadcasted_iota(jnp.int32, (6, 8, 128), 1) + (4 * s - 1)
    inside = (plane >= 0) & (plane < 16) & (row >= 0) & (row < 256)
    grown[...] = jnp.zeros_like(grown)
    for t in range(4):
        value = lax.dot_general(
            spread[t], p2[...], (((1,), (1,)), ((), ())), preferred_element_type=F32
        ).reshape(6, 8, 128)
        value = jnp.where(inside, jnp.maximum(value, 0.0), 0.0)
        for p in range(6):
            grown[pl.ds(8, 8, stride=2), :] = value[p]
            grown[pl.ds(9, 8, stride=2), :] = value[p]
            for dz in range(3):
                rows = grown[pl.ds(5 + dz, 16), :].astype(BF)
                ups[dz, 2 * p, :, 128 * t : 128 * t + 128] = rows
                ups[dz, 2 * p + 1, :, 128 * t : 128 * t + 128] = rows

    for g in range(2):
        acc[0:10, :, 256 * g : 256 * g + 256] = convolve(
            [(ups, w5u), (sides, w5s)], 10, 16, g
        )

    @pl.loop(0, 10, unroll=5)
    def _(p):
        x = 8 * q - 1 + p
        inside = row_mask(16, 8 * s - 4, 512) & (x >= 0) & (x < 32)
        value = jnp.where(inside, jnp.maximum(acc[p], 0.0), 0.0)
        for t in range(4):
            tall[t, pl.ds(0, 16, stride=2), :] = value[:, 128 * t : 128 * t + 128]
            tall[t, pl.ds(1, 16, stride=2), :] = value[:, 128 * t : 128 * t + 128]
        for dz in range(3):
            rows = jnp.concatenate([tall[t, pl.ds(7 + dz, 16), :] for t in range(4)], axis=1).astype(BF)
            fine[dz, 2 * p] = rows
            fine[dz, 2 * p + 1] = rows

    for g in range(2):
        total = convolve([(fine.at[:, 1:19], w6u)], 16, 16, g)
        total = (total + skip_part[:, :, 256 * g : 256 * g + 256]).astype(BF)
        for i in range(4):
            for j in range(2):
                out[i, 2 * g + j] = total[4 * i : 4 * i + 4, :, 128 * j : 128 * j + 128]


def call(kernel, outs, scratch=(), flops=0, limit=8):
    whole = pl.BlockSpec(memory_space=pltpu.VMEM)

    def run(*args):
        return pl.pallas_call(
            kernel,
            out_shape=outs,
            in_specs=[whole] * len(args),
            out_specs=jax.tree.map(lambda _: whole, outs),
            scratch_shapes=list(scratch),
            compiler_params=pltpu.CompilerParams(vmem_limit_bytes=limit << 20),
            cost_estimate=pl.CostEstimate(flops=flops, bytes_accessed=4 << 20, transcendentals=0),
        )(*args)

    return run


def shape(*dims):
    return jax.ShapeDtypeStruct(dims, BF)


def local(
    features, conv_one, conv_two, conv_three, conv_four, depth_one, point_one, depth_two, point_two,
    conv_five, conv_six,
):
    taps_one = jnp.pad(depth_one.astype(F32).T, ((0, 5), (0, 64)))
    taps_two = jnp.pad(depth_two.astype(F32).T, ((0, 5), (0, 0)))
    mix_one = jnp.pad(point_one, ((0, 0), (0, 64)))
    bands = shape(9, 512, 256)

    rows = call(to_rows_kernel, shape(16, 4, 16, 128))(features.reshape(512, 256))
    own = lax.all_to_all(rows, PLANE, 0, 0, tiled=True, axis_index_groups=GROUPS)
    own = own.reshape(4, 4, 4, 16, 128)
    w1, w2, w3, w4 = call(encoder_weights_kernel, (bands,) * 4, limit=LIMITS[0])(
        conv_one, conv_two, conv_three, conv_four
    )
    w5u, w5s, w6u, w6s = call(decoder_weights_kernel, (bands,) * 4, limit=LIMITS[1])(conv_five, conv_six)
    q, s = position()
    x_swaps = [swap_pairs(1, 0, parity) for parity in range(2)]
    z_swaps = [swap_pairs(0, 1, parity) for parity in range(2)]
    x_got = []
    for turn in range(2):
        start = jnp.where((q + turn) % 2 == 0, 2, 0)
        piece = lax.dynamic_slice_in_dim(own, start, 2, 0)
        x_got.append(lax.ppermute(piece, EVERY, x_swaps[turn]))
    broad = jnp.concatenate([x_got[0], own, x_got[1]], axis=0)
    z_got = []
    for turn in range(2):
        piece = jnp.where((s + turn) % 2 == 0, broad[..., 8:16, :], broad[..., 0:8, :])
        z_got.append(lax.ppermute(piece, EVERY, z_swaps[turn]))
    own_first = call(
        own_rows_kernel,
        shape(26, 16, 512),
        [
            pltpu.VMEM((32, 16, 512), F32),
            pltpu.VMEM((3, 28, 16, 512), BF),
            pltpu.VMEM((26, 16, 512), F32),
        ],
        flops=3 << 30,
        limit=16,
    )(own, *x_got, w1)
    skip, half_skip = call(
        encoder_kernel,
        (shape(3, 19, 16, 512), shape(8, 8, 512)),
        [
            pltpu.VMEM((32, 32, 512), F32),
            pltpu.VMEM((3, 28, 16, 512), BF),
            pltpu.VMEM((2, 32, 512), F32),
            pltpu.VMEM((3, 26, 32, 512), BF),
            pltpu.VMEM((26, 32, 512), F32),
            pltpu.VMEM((3, 12, 16, 512), BF),
            pltpu.VMEM((3, 10, 16, 512), BF),
            pltpu.VMEM((4, 4, 32, 128), F32),
        ],
        flops=6 << 30,
        limit=LIMITS[2],
    )(own, *x_got, *z_got, own_first, w1, w2, w3, w4)
    x_got = []
    for turn in range(2):
        start = jnp.where((q + turn) % 2 == 0, 2, 0)
        piece = lax.dynamic_slice_in_dim(half_skip, start, 6, 0)
        x_got.append(lax.ppermute(piece, EVERY, x_swaps[turn]))
    broad = jnp.concatenate([x_got[0], half_skip, x_got[1]], axis=0)
    z_got = [lax.ppermute(broad, EVERY, z_swaps[turn]) for turn in range(2)]
    skip_part = call(
        skip_kernel, jax.ShapeDtypeStruct((16, 16, 512), F32), flops=2 << 30, limit=12
    )(skip, w6s)
    rows = call(
        decoder_kernel,
        shape(4, 4, 4, 16, 128),
        [
            pltpu.VMEM((20, 24, 512), F32),
            pltpu.VMEM((3, 12, 16, 512), BF),
            pltpu.VMEM((32, 128), F32),
            pltpu.VMEM((10, 16, 512), F32),
            pltpu.VMEM((8, 16, 512), F32),
            pltpu.VMEM((32, 128), F32),
            pltpu.VMEM((3, 12, 16, 512), BF),
            pltpu.VMEM((16, 16, 512), F32),
            pltpu.VMEM((4, 32, 128), F32),
            pltpu.VMEM((3, 20, 16, 512), BF),
        ],
        flops=2 << 30,
        limit=LIMITS[3],
    )(
        half_skip, *x_got, *z_got, skip_part,
        taps_one, mix_one, taps_two, point_two, w5u, w5s, w6u,
    )
    back = lax.all_to_all(
        rows.reshape(16, 4, 16, 128), PLANE, 0, 0, tiled=True, axis_index_groups=GROUPS
    )
    return call(from_rows_kernel, shape(512, 256))(back).reshape(32, 4, 4, 256)


def solution(mesh):
    in_specs = (P(None, "gx", "gy", "gz"), P(), P(), P(), P(), P(), P(), P(), P(), P(), P())
    out_specs = P(None, "gx", "gy", "gz")
    return jax.shard_map(local, mesh=mesh, in_specs=in_specs, out_specs=out_specs, check_vma=False)
```

```python
import jax
import jax.numpy as jnp
from jax import lax
from jax.experimental import pallas as pl
from jax.experimental.pallas import tpu as pltpu
from jax.sharding import PartitionSpec as P


BF = jnp.bfloat16
F32 = jnp.float32
PLANE = ("gx", "gy")
EVERY = ("gx", "gy", "gz")
LIMITS = (24, 24, 32, 32)


def slab_at(z_low, across, core):
    step = across + z_low * (3 - 2 * across)
    return 8 * z_low + 2 * step + (core + step) % 2


SLABS = [slab_at(rank // 8, rank % 4, rank // 4 % 2) for rank in range(16)]


def device_at(q, slab, k):
    rank = SLABS.index(slab)
    return ((q * 4 + rank // 4) * 4 + rank % 4) * 4 + k


def swap_pairs(step_x, step_z, parity):
    pairs = []
    for q in range(4):
        for s in range(64):
            to_q, to_s = q + step_x, s + step_z
            if (q * step_x + s * step_z) % 2 == parity and to_q < 4 and to_s < 64:
                here = device_at(q, s % 16, s // 16)
                there = device_at(to_q, to_s % 16, to_s // 16)
                pairs += [(here, there), (there, here)]
    return pairs


GROUPS = [list(range(16 * q, 16 * q + 16)) for q in range(4)]


def position():
    gx, gy, gz = lax.axis_index("gx"), lax.axis_index("gy"), lax.axis_index("gz")
    return gx // 4, gz * 16 + slab_at(gx // 2 % 2, gy, gx % 2)


def identity():
    row = lax.broadcasted_iota(jnp.int32, (128, 128), 0)
    lane = lax.broadcasted_iota(jnp.int32, (128, 128), 1)
    return jnp.where(row == lane, 1.0, 0.0).astype(BF)


def to_rows_kernel(cells_ref, out_ref):
    same = identity()
    for x in range(4):
        cells = jnp.concatenate([cells_ref[:, x, y, :] for y in range(4)], axis=0)
        turned = lax.dot_general(
            cells, same, (((0,), (0,)), ((), ())), preferred_element_type=F32
        ).astype(BF)
        for rank, slab in enumerate(SLABS):
            out_ref[rank, x] = turned[16 * slab : 16 * slab + 16]


def from_rows_kernel(rows_ref, out_ref):
    same = identity()
    for x in range(4):
        rows = jnp.concatenate([rows_ref[SLABS.index(slab), x] for slab in range(16)], axis=0)
        turned = lax.dot_general(
            same, rows, (((1,), (1,)), ((), ())), preferred_element_type=F32
        ).astype(BF)
        for y in range(4):
            out_ref[:, x, y, :] = turned[32 * y : 32 * y + 32]


def band(spread, out_ref, stride, first, used, lanes_in, lanes_out, grown=False):
    per_tile = 128 // lanes_out
    lead = 128 // lanes_in
    group = lax.broadcasted_iota(jnp.int32, (used, 128), 1) // lanes_out
    chosen = [jnp.where(group == j, 1.0, 0.0).astype(BF) for j in range(per_tile)]
    empty = jnp.zeros((lanes_in, 128), BF)
    for dx in range(3):
        for dz in range(3):
            tap = dx * 3 + dz
            parts = []
            for dy in range(3):
                start = ((dx * 3 + dy) * 3 + dz) * stride + first
                parts.append(spread[start : start + used, :])
            if grown:
                pieces = {-1: parts[2], 0: parts[1] + parts[2], 1: parts[0] + parts[1], 2: parts[0]}
            else:
                pieces = {1: parts[0], 0: parts[1], -1: parts[2]}
            pieces = {gap: piece.astype(BF) for gap, piece in pieces.items()}
            made = {}
            for at in range(out_ref.shape[1] // lanes_in):
                for tile in range(2):
                    key = (2 if grown else 1) * (at - lead) - per_tile * tile
                    if key not in made:
                        block = None
                        for gap, piece in pieces.items():
                            if 0 <= key + gap < per_tile:
                                term = piece * chosen[key + gap]
                                block = term if block is None else block + term
                        made[key] = block
                    block = made[key]
                    lanes = slice(128 * tile, 128 * tile + 128)
                    if block is None:
                        out_ref[tap, at * lanes_in : (at + 1) * lanes_in, lanes] = empty
                    else:
                        out_ref[tap, at * lanes_in : at * lanes_in + used, lanes] = block
                        if used < lanes_in:
                            out_ref[tap, at * lanes_in + used : (at + 1) * lanes_in, lanes] = empty[
                                : lanes_in - used
                            ]


def spread_lanes(weight, lanes_out):
    outs = weight.shape[0]
    row = lax.broadcasted_iota(jnp.int32, (outs, 128), 0)
    lane = lax.broadcasted_iota(jnp.int32, (outs, 128), 1)
    chosen = jnp.where(lane % lanes_out == row, 1.0, 0.0).astype(BF)
    return lax.dot_general(weight, chosen, (((0,), (0,)), ((), ())), preferred_element_type=F32)


def encoder_weights_kernel(w1, w2, w3, w4, o1, o2, o3, o4):
    band(spread_lanes(w1[...], 32), o1, 32, 0, 32, 32, 32)
    band(spread_lanes(w2[...], 32), o2, 32, 0, 32, 32, 32)
    band(spread_lanes(w3[...], 64), o3, 32, 0, 32, 64, 64)
    band(spread_lanes(w4[...], 64), o4, 64, 0, 64, 64, 64)


def decoder_weights_kernel(w5, w6, d1, d2, o5u, o5s, o6u, o6s, taps_one, taps_two):
    wide = spread_lanes(w5[...], 64)
    band(wide, o5u, 192, 0, 128, 128, 64, grown=True)
    band(wide, o5s, 192, 128, 64, 64, 64)
    fine = spread_lanes(w6[...], 32)
    band(fine, o6u, 96, 0, 64, 64, 32, grown=True)
    band(fine, o6s, 96, 64, 32, 32, 32)
    for taps, weight in ((taps_one, d1), (taps_two, d2)):
        same = identity()[: weight.shape[0]]
        taps[...] = lax.dot_general(
            weight[...], same, (((0,), (0,)), ((), ())), preferred_element_type=F32
        )


def convolve(terms, planes, rows, g):
    taps = [
        (field[dz, dx : dx + planes, :, 128 * g : 128 * g + 384].reshape(planes * rows, 384),
         weights[dx * 3 + dz, 128 * (1 - g) : 128 * (1 - g) + 384, :])
        for field, weights in terms
        for dx in range(3)
        for dz in range(3)
    ]
    total = None
    for at in range(0, len(taps), 2):
        left = [left for left, _ in taps[at : at + 2]]
        right = [right for _, right in taps[at : at + 2]]
        part = jnp.dot(
            jnp.concatenate(left, axis=1), jnp.concatenate(right, axis=0), preferred_element_type=F32
        )
        total = part if total is None else total + part
    return total.reshape(planes, rows, 256)


def row_mask(rows, start, limit):
    at = lax.broadcasted_iota(jnp.int32, (rows, 512), 0) + start
    return (at >= 0) & (at < limit)


def store_turned(dest, plane, value, keep=slice(None)):
    dest[0, plane] = pltpu.roll(value, 1, 0)[keep].astype(BF)
    dest[1, plane] = value[keep].astype(BF)
    dest[2, plane] = pltpu.roll(value, value.shape[0] - 1, 0)[keep].astype(BF)


def pick_x_kernel(own, out_1, out_2):
    q, _ = position()

    def fill(out, start):
        for p in range(6):
            out[p] = own[(start + p) // 4, :, (start + p) % 4]

    @pl.when(q % 2 == 0)
    def _():
        fill(out_1, 10)
        fill(out_2, 0)

    @pl.when(q % 2 == 1)
    def _():
        fill(out_1, 0)
        fill(out_2, 10)


def pick_z_kernel(own, x1, x2, out_1, out_2):
    _, s = position()

    def fill(out, rows):
        out[0:6] = x1[:, :, rows]
        for x in range(16):
            out[6 + x] = own[x // 4, :, x % 4, rows]
        out[22:28] = x2[:, :, rows]

    @pl.when(s % 2 == 0)
    def _():
        fill(out_1, slice(8, 16))
        fill(out_2, slice(0, 8))

    @pl.when(s % 2 == 1)
    def _():
        fill(out_1, slice(0, 8))
        fill(out_2, slice(8, 16))


def join_kernel(own, x1, x2, out):
    out[0:6] = x1[...]
    out[6:14] = own[...]
    out[14:20] = x2[...]


def x_blocks(own, x1, x2, q):
    plane_1 = 22 * (1 - q % 2)
    blocks = [(pl.ds(plane_1, 6), lambda j: x1[:, j], 0), (pl.ds(22 - plane_1, 6), lambda j: x2[:, j], 22)]
    for i in range(4):
        blocks.append((slice(6 + 4 * i, 10 + 4 * i), lambda j, i=i: own[i, j], 6 + 4 * i))
    return blocks


def own_rows_kernel(own, x1, x2, w1, w2, own_first, own_skip, field, turned, acc):
    q, _ = position()
    for planes, source, _ in x_blocks(own, x1, x2, q):
        for j in range(4):
            field[planes, :, 128 * j : 128 * j + 128] = source(j).astype(F32)

    @pl.loop(0, 28, unroll=4)
    def _(p):
        store_turned(turned, p, field[p])

    for g in range(2):
        acc[:, :, 256 * g : 256 * g + 256] = convolve([(turned, w1)], 26, 16, g)

    @pl.loop(0, 26, unroll=2)
    def _(p):
        x = 16 * q - 5 + p
        value = jnp.where((x >= 0) & (x < 64), jnp.maximum(acc[p], 0.0), 0.0)
        own_first[p] = value.astype(BF)
        store_turned(turned, p, value)

    for g in range(2):
        acc[0:24, :, 256 * g : 256 * g + 256] = convolve([(turned, w2)], 24, 16, g)

    @pl.loop(0, 24, unroll=4)
    def _(p):
        x = 16 * q - 4 + p
        own_skip[p] = jnp.where((x >= 0) & (x < 64), jnp.maximum(acc[p], 0.0), 0.0).astype(BF)


def rim_rows_inside(low, high):
    row = lax.broadcasted_iota(jnp.int32, (16, 512), 0)
    row = jnp.where(row < 8, row + low, row + (high - 8))
    return (row >= 0) & (row < 1024)


def encoder_kernel(
    own, x1, x2, z1, z2, own_first, own_skip, w1, w2, w3, w4,
    skip_out, half_out, half_1, half_2, field, turned, full, acc, half, mid, pooled,
):
    q, s = position()
    x0, z0 = 16 * q, 16 * s
    row_1 = pl.multiple_of(24 * (1 - s % 2), 8)
    row_2 = pl.multiple_of(24 * (s % 2), 8)
    for planes, source, at in x_blocks(own, x1, x2, q):
        for j in range(4):
            lanes = slice(128 * j, 128 * j + 128)
            cells = source(j)
            count = cells.shape[0]
            field[planes, 8:24, lanes] = cells.astype(F32)
            field[planes, pl.ds(row_1, 8), lanes] = z1[at : at + count, j].astype(F32)
            field[planes, pl.ds(row_2, 8), lanes] = z2[at : at + count, j].astype(F32)

    @pl.loop(0, 28, unroll=4)
    def _(p):
        for dz in range(3):
            turned[dz, p] = jnp.concatenate(
                [field[p, pl.ds(dz, 8), :], field[p, pl.ds(22 + dz, 8), :]], axis=0
            ).astype(BF)

    for g in range(2):
        acc[:, :, 256 * g : 256 * g + 256] = convolve([(turned, w1)], 26, 16, g)

    for slot in range(4):
        full[slot, 0:8] = jnp.zeros((8, 512), F32)
        full[slot, 24:32] = jnp.zeros((8, 512), F32)
    inside = rim_rows_inside(z0 - 7, z0 + 15)

    @pl.loop(0, 26, unroll=2)
    def _(p):
        x = x0 - 5 + p
        value = jnp.where(inside & (x >= 0) & (x < 64), jnp.maximum(acc[p], 0.0), 0.0)
        slot = p % 2
        full[slot, 8:24] = own_first[p].astype(F32)
        full[slot, 1:9] = value[0:8]
        full[slot, 23:31] = value[8:16]
        for dz in range(3):
            turned[dz, p] = jnp.concatenate(
                [full[slot, pl.ds(1 + dz, 8), :], full[slot, pl.ds(21 + dz, 8), :]], axis=0
            ).astype(BF)

    for g in range(2):
        acc[0:24, :, 256 * g : 256 * g + 256] = convolve([(turned, w2)], 24, 16, g)

    for slot in range(4):
        full[slot, 0:8] = jnp.zeros((8, 512), F32)
        full[slot, 24:32] = jnp.zeros((8, 512), F32)
    inside_two = rim_rows_inside(z0 - 6, z0 + 14)

    @pl.loop(0, 12, unroll=4)
    def _(h):
        best = None
        for b in range(2):
            p = 2 * h + b
            x = x0 - 4 + p
            rim = jnp.where(inside_two & (x >= 0) & (x < 64), jnp.maximum(acc[p], 0.0), 0.0)
            slot = 2 * (h % 2) + b
            full[slot, 8:24] = own_skip[p].astype(F32)
            full[slot, 2:10] = rim[0:8]
            full[slot, 22:30] = rim[8:16]
            value = full[slot]
            store_turned(skip_out, jnp.where((p >= 3) & (p < 21), p - 3, 18), value, slice(8, 24))
            best = value if best is None else jnp.maximum(best, value)
        best = jnp.maximum(best, pltpu.roll(best, 480, 1))
        pieces = []
        for t in range(4):
            pooled[h % 4, t] = best[:, 128 * t : 128 * t + 128]
            pieces.append(
                jnp.maximum(
                    pooled[h % 4, t, pl.ds(0, 16, stride=2), :], pooled[h % 4, t, pl.ds(1, 16, stride=2), :]
                )
            )
        store_turned(half, h, jnp.concatenate(pieces, axis=1))

    for g in range(2):
        acc[0:10, 0:16, 256 * g : 256 * g + 256] = convolve([(half, w3)], 10, 16, g)

    @pl.loop(0, 10, unroll=5)
    def _(p):
        x = 8 * q - 1 + p
        inside = row_mask(16, 8 * s - 4, 512) & (x >= 0) & (x < 32)
        store_turned(mid, p, jnp.where(inside, jnp.maximum(acc[p, 0:16], 0.0), 0.0))

    for g in range(2):
        acc[0:8, 0:16, 256 * g : 256 * g + 256] = convolve([(mid, w4)], 8, 16, g)
    half_out[...] = jnp.maximum(acc[0:8, 4:12, :], 0.0).astype(BF)

    @pl.when(q % 2 == 0)
    def _():
        half_1[...] = half_out[2:8]
        half_2[...] = half_out[0:6]

    @pl.when(q % 2 == 1)
    def _():
        half_1[...] = half_out[0:6]
        half_2[...] = half_out[2:8]


def skip_kernel(skip, w6s, out):
    for g in range(2):
        out[:, :, 256 * g : 256 * g + 256] = convolve([(skip.at[:, 0:18], w6s)], 16, 16, g)


def depthwise(source, taps, planes, offset):
    sums = []
    for t in range(4):
        total = jnp.zeros((planes, 8, 128), F32)
        for dx in range(3):
            for dy in range(3):
                at = t + dy - 1
                if not 0 <= at < 4:
                    continue
                for dz in range(3):
                    tap = (dx * 3 + dy) * 3 + dz
                    factor = taps[tap : tap + 1, :].reshape(1, 1, 128)
                    total += (
                        source[dx : dx + planes, pl.ds(offset + dz, 8), 128 * at : 128 * at + 128]
                        * factor
                    )
        sums.append(total.reshape(planes * 8, 128).astype(BF))
    return sums


def decoder_kernel(
    own, x1, x2, z1, z2, skip_part, d1, p1, d2, p2, w5u, w5s, w6u,
    out, whole, sides, pooled, quarter, mixed, grown, ups, acc, tall, fine,
):
    q, s = position()
    plane_1 = 14 * (1 - q % 2)
    plane_2 = 14 - plane_1
    row_1 = pl.multiple_of(16 * (1 - s % 2), 8)
    row_2 = pl.multiple_of(16 * (s % 2), 8)
    for start, size, source, at in ((plane_1, 6, x1, 0), (6, 8, own, 6), (plane_2, 6, x2, 14)):
        whole[pl.ds(start, size), 8:16, :] = source[...].astype(F32)
        whole[pl.ds(start, size), pl.ds(row_1, 8), :] = z1[at : at + size].astype(F32)
        whole[pl.ds(start, size), pl.ds(row_2, 8), :] = z2[at : at + size].astype(F32)

    @pl.loop(0, 12, unroll=4)
    def _(p):
        for dz in range(3):
            sides[dz, p] = whole[p + 4, pl.ds(3 + dz, 16), :].astype(BF)

    quarter[...] = jnp.zeros_like(quarter)

    @pl.loop(0, 10, unroll=5)
    def _(p):
        best = jnp.maximum(whole[2 * p], whole[2 * p + 1])
        best = jnp.maximum(best, pltpu.roll(best, 448, 1))
        for t in range(4):
            pooled[0:24, :] = best[:, 128 * t : 128 * t + 128]
            quarter[p, 0:12, 128 * t : 128 * t + 128] = jnp.maximum(
                pooled[pl.ds(0, 12, stride=2), :], pooled[pl.ds(1, 12, stride=2), :]
            )

    mixed[...] = jnp.zeros_like(mixed)
    spread = depthwise(quarter, d1, 8, 1)
    plane = lax.broadcasted_iota(jnp.int32, (8, 8, 128), 0) + (4 * q - 2)
    row = lax.broadcasted_iota(jnp.int32, (8, 8, 128), 1) + (4 * s - 2)
    inside = (plane >= 0) & (plane < 16) & (row >= 0) & (row < 256)
    for t in range(4):
        value = lax.dot_general(
            spread[t][:, :64], p1[...], (((1,), (1,)), ((), ())), preferred_element_type=F32
        ).reshape(8, 8, 128)
        value = jnp.where(inside, jnp.maximum(value, 0.0), 0.0)
        mixed[:, 0:8, 128 * t : 128 * t + 128] = value.astype(BF).astype(F32)

    spread = depthwise(mixed, d2, 6, 0)
    plane = lax.broadcasted_iota(jnp.int32, (6, 8, 128), 0) + (4 * q - 1)
    row = lax.broadcasted_iota(jnp.int32, (6, 8, 128), 1) + (4 * s - 1)
    inside = (plane >= 0) & (plane < 16) & (row >= 0) & (row < 256)
    grown[...] = jnp.zeros_like(grown)
    for t in range(4):
        value = lax.dot_general(
            spread[t], p2[...], (((1,), (1,)), ((), ())), preferred_element_type=F32
        ).reshape(6, 8, 128)
        value = jnp.where(inside, jnp.maximum(value, 0.0), 0.0)
        for p in range(6):
            grown[pl.ds(8, 8, stride=2), :] = value[p]
            grown[pl.ds(9, 8, stride=2), :] = value[p]
            for dz in range(3):
                rows = grown[pl.ds(5 + dz, 16), :].astype(BF)
                ups[dz, 2 * p, :, 128 * t : 128 * t + 128] = rows
                ups[dz, 2 * p + 1, :, 128 * t : 128 * t + 128] = rows

    for g in range(2):
        acc[0:10, :, 256 * g : 256 * g + 256] = convolve(
            [(ups, w5u), (sides, w5s)], 10, 16, g
        )

    @pl.loop(0, 10, unroll=5)
    def _(p):
        x = 8 * q - 1 + p
        inside = row_mask(16, 8 * s - 4, 512) & (x >= 0) & (x < 32)
        value = jnp.where(inside, jnp.maximum(acc[p], 0.0), 0.0)
        for t in range(4):
            tall[t, pl.ds(0, 16, stride=2), :] = value[:, 128 * t : 128 * t + 128]
            tall[t, pl.ds(1, 16, stride=2), :] = value[:, 128 * t : 128 * t + 128]
        for dz in range(3):
            rows = jnp.concatenate([tall[t, pl.ds(7 + dz, 16), :] for t in range(4)], axis=1).astype(BF)
            fine[dz, 2 * p] = rows
            fine[dz, 2 * p + 1] = rows

    for g in range(2):
        total = convolve([(fine.at[:, 1:19], w6u)], 16, 16, g)
        total = (total + skip_part[:, :, 256 * g : 256 * g + 256]).astype(BF)
        for i in range(4):
            for j in range(2):
                out[i, 2 * g + j] = total[4 * i : 4 * i + 4, :, 128 * j : 128 * j + 128]


def call(kernel, outs, scratch=(), flops=0, limit=8):
    whole = pl.BlockSpec(memory_space=pltpu.VMEM)

    def run(*args):
        return pl.pallas_call(
            kernel,
            out_shape=outs,
            in_specs=[whole] * len(args),
            out_specs=jax.tree.map(lambda _: whole, outs),
            scratch_shapes=list(scratch),
            compiler_params=pltpu.CompilerParams(vmem_limit_bytes=limit << 20),
            cost_estimate=pl.CostEstimate(flops=flops, bytes_accessed=4 << 20, transcendentals=0),
        )(*args)

    return run


def shape(*dims):
    return jax.ShapeDtypeStruct(dims, BF)


def forward(
    features, conv_one, conv_two, conv_three, conv_four, depth_one, point_one, depth_two, point_two,
    conv_five, conv_six,
):
    bands = shape(9, 512, 256)

    rows = call(to_rows_kernel, shape(16, 4, 16, 128))(features)
    own = lax.all_to_all(rows, PLANE, 0, 0, tiled=True, axis_index_groups=GROUPS)
    own = own.reshape(4, 4, 4, 16, 128)
    w1, w2, w3, w4 = call(encoder_weights_kernel, (bands,) * 4, limit=LIMITS[0])(
        conv_one, conv_two, conv_three, conv_four
    )
    taps = jax.ShapeDtypeStruct((27, 128), F32)
    w5u, w5s, w6u, w6s, taps_one, taps_two = call(
        decoder_weights_kernel, (bands,) * 4 + (taps,) * 2, limit=LIMITS[1]
    )(conv_five, conv_six, depth_one, depth_two)
    x_swaps = [swap_pairs(1, 0, parity) for parity in range(2)]
    z_swaps = [swap_pairs(0, 1, parity) for parity in range(2)]
    pieces = call(pick_x_kernel, (shape(6, 4, 16, 128),) * 2, flops=8 << 30)(own)
    x_got = [lax.ppermute(piece, EVERY, pairs) for piece, pairs in zip(pieces, x_swaps)]
    pieces = call(pick_z_kernel, (shape(28, 4, 8, 128),) * 2)(own, *x_got)
    z_got = [lax.ppermute(piece, EVERY, pairs) for piece, pairs in zip(pieces, z_swaps)]
    own_first, own_skip = call(
        own_rows_kernel,
        (shape(26, 16, 512), shape(24, 16, 512)),
        [
            pltpu.VMEM((28, 16, 512), F32),
            pltpu.VMEM((3, 28, 16, 512), BF),
            pltpu.VMEM((26, 16, 512), F32),
        ],
        flops=3 << 30,
        limit=16,
    )(own, *x_got, w1, w2)
    skip, half_skip, *pieces = call(
        encoder_kernel,
        (shape(3, 19, 16, 512), shape(8, 8, 512), shape(6, 8, 512), shape(6, 8, 512)),
        [
            pltpu.VMEM((28, 32, 512), F32),
            pltpu.VMEM((3, 28, 16, 512), BF),
            pltpu.VMEM((4, 32, 512), F32),
            pltpu.VMEM((26, 16, 512), F32),
            pltpu.VMEM((3, 12, 16, 512), BF),
            pltpu.VMEM((3, 10, 16, 512), BF),
            pltpu.VMEM((4, 4, 32, 128), F32),
        ],
        flops=6 << 30,
        limit=LIMITS[2],
    )(own, *x_got, *z_got, own_first, own_skip, w1, w2, w3, w4)
    x_got = []
    for turn in range(2):
        x_got.append(lax.ppermute(pieces[turn], EVERY, x_swaps[turn]))
    broad = call(join_kernel, shape(20, 8, 512))(half_skip, *x_got)
    z_got = [lax.ppermute(broad, EVERY, pairs) for pairs in z_swaps]
    skip_part = call(
        skip_kernel, jax.ShapeDtypeStruct((16, 16, 512), F32), flops=2 << 30, limit=12
    )(skip, w6s)
    rows = call(
        decoder_kernel,
        shape(4, 4, 4, 16, 128),
        [
            pltpu.VMEM((20, 24, 512), F32),
            pltpu.VMEM((3, 12, 16, 512), BF),
            pltpu.VMEM((32, 128), F32),
            pltpu.VMEM((10, 16, 512), F32),
            pltpu.VMEM((8, 16, 512), F32),
            pltpu.VMEM((32, 128), F32),
            pltpu.VMEM((3, 12, 16, 512), BF),
            pltpu.VMEM((16, 16, 512), F32),
            pltpu.VMEM((4, 32, 128), F32),
            pltpu.VMEM((3, 20, 16, 512), BF),
        ],
        flops=2 << 30,
        limit=LIMITS[3],
    )(
        half_skip, *x_got, *z_got, skip_part,
        taps_one, point_one, taps_two, point_two, w5u, w5s, w6u,
    )
    back = lax.all_to_all(
        rows.reshape(16, 4, 16, 128), PLANE, 0, 0, tiled=True, axis_index_groups=GROUPS
    )
    return call(from_rows_kernel, shape(32, 4, 4, 256))(back)


def solution(mesh):
    in_specs = (P(None, "gx", "gy", "gz"), P(), P(), P(), P(), P(), P(), P(), P(), P(), P())
    out_specs = P(None, "gx", "gy", "gz")
    return jax.shard_map(forward, mesh=mesh, in_specs=in_specs, out_specs=out_specs, check_vma=False)
```

```python
import jax
import jax.numpy as jnp
from jax import lax
from jax.experimental import pallas as pl
from jax.experimental.pallas import tpu as pltpu
from jax.sharding import PartitionSpec as P


BF = jnp.bfloat16
F32 = jnp.float32
PLANE = ("gx", "gy")
EVERY = ("gx", "gy", "gz")
LIMITS = (24, 24, 32, 32)


def slab_at(z_low, across, core):
    step = across + z_low * (3 - 2 * across)
    return 8 * z_low + 2 * step + (core + step) % 2


SLABS = [slab_at(rank // 8, rank % 4, rank // 4 % 2) for rank in range(16)]


def device_at(q, slab, k):
    rank = SLABS.index(slab)
    return ((q * 4 + rank // 4) * 4 + rank % 4) * 4 + k


def swap_pairs(step_x, step_z, parity):
    pairs = []
    for q in range(4):
        for s in range(64):
            to_q, to_s = q + step_x, s + step_z
            if (q * step_x + s * step_z) % 2 == parity and to_q < 4 and to_s < 64:
                here = device_at(q, s % 16, s // 16)
                there = device_at(to_q, to_s % 16, to_s // 16)
                pairs += [(here, there), (there, here)]
    return pairs


GROUPS = [list(range(16 * q, 16 * q + 16)) for q in range(4)]


def position():
    gx, gy, gz = lax.axis_index("gx"), lax.axis_index("gy"), lax.axis_index("gz")
    return gx // 4, gz * 16 + slab_at(gx // 2 % 2, gy, gx % 2)


def identity():
    row = lax.broadcasted_iota(jnp.int32, (128, 128), 0)
    lane = lax.broadcasted_iota(jnp.int32, (128, 128), 1)
    return jnp.where(row == lane, 1.0, 0.0).astype(BF)


def to_rows_kernel(cells_ref, out_ref):
    same = identity()
    for x in range(4):
        cells = jnp.concatenate([cells_ref[:, x, y, :] for y in range(4)], axis=0)
        turned = lax.dot_general(
            cells, same, (((0,), (0,)), ((), ())), preferred_element_type=F32
        ).astype(BF)
        for rank, slab in enumerate(SLABS):
            out_ref[rank, x] = turned[16 * slab : 16 * slab + 16]


def from_rows_kernel(rows_ref, out_ref):
    same = identity()
    for x in range(4):
        rows = jnp.concatenate([rows_ref[SLABS.index(slab), x] for slab in range(16)], axis=0)
        turned = lax.dot_general(
            same, rows, (((1,), (1,)), ((), ())), preferred_element_type=F32
        ).astype(BF)
        for y in range(4):
            out_ref[:, x, y, :] = turned[32 * y : 32 * y + 32]


def band(spread, out_ref, stride, first, used, lanes_in, lanes_out, grown=False):
    per_tile = 128 // lanes_out
    lead = 128 // lanes_in
    group = lax.broadcasted_iota(jnp.int32, (used, 128), 1) // lanes_out
    chosen = [jnp.where(group == j, 1.0, 0.0).astype(BF) for j in range(per_tile)]
    empty = jnp.zeros((lanes_in, 128), BF)
    for dx in range(3):
        for dz in range(3):
            tap = dx * 3 + dz
            parts = []
            for dy in range(3):
                start = ((dx * 3 + dy) * 3 + dz) * stride + first
                parts.append(spread[start : start + used, :])
            if grown:
                pieces = {-1: parts[2], 0: parts[1] + parts[2], 1: parts[0] + parts[1], 2: parts[0]}
            else:
                pieces = {1: parts[0], 0: parts[1], -1: parts[2]}
            pieces = {gap: piece.astype(BF) for gap, piece in pieces.items()}
            made = {}
            for at in range(out_ref.shape[1] // lanes_in):
                for tile in range(2):
                    key = (2 if grown else 1) * (at - lead) - per_tile * tile
                    if key not in made:
                        block = None
                        for gap, piece in pieces.items():
                            if 0 <= key + gap < per_tile:
                                term = piece * chosen[key + gap]
                                block = term if block is None else block + term
                        made[key] = block
                    block = made[key]
                    lanes = slice(128 * tile, 128 * tile + 128)
                    if block is None:
                        out_ref[tap, at * lanes_in : (at + 1) * lanes_in, lanes] = empty
                    else:
                        out_ref[tap, at * lanes_in : at * lanes_in + used, lanes] = block
                        if used < lanes_in:
                            out_ref[tap, at * lanes_in + used : (at + 1) * lanes_in, lanes] = empty[
                                : lanes_in - used
                            ]


def spread_lanes(weight, lanes_out):
    outs = weight.shape[0]
    row = lax.broadcasted_iota(jnp.int32, (outs, 128), 0)
    lane = lax.broadcasted_iota(jnp.int32, (outs, 128), 1)
    chosen = jnp.where(lane % lanes_out == row, 1.0, 0.0).astype(BF)
    return lax.dot_general(weight, chosen, (((0,), (0,)), ((), ())), preferred_element_type=F32)


def encoder_weights_kernel(w1, w2, w3, w4, o1, o2, o3, o4):
    band(spread_lanes(w1[...], 32), o1, 32, 0, 32, 32, 32)
    band(spread_lanes(w2[...], 32), o2, 32, 0, 32, 32, 32)
    band(spread_lanes(w3[...], 64), o3, 32, 0, 32, 64, 64)
    band(spread_lanes(w4[...], 64), o4, 64, 0, 64, 64, 64)


def decoder_weights_kernel(w5, w6, d1, d2, o5u, o5s, o6u, o6s, taps_one, taps_two):
    wide = spread_lanes(w5[...], 64)
    band(wide, o5u, 192, 0, 128, 128, 64, grown=True)
    band(wide, o5s, 192, 128, 64, 64, 64)
    fine = spread_lanes(w6[...], 32)
    band(fine, o6u, 96, 0, 64, 64, 32, grown=True)
    band(fine, o6s, 96, 64, 32, 32, 32)
    for taps, weight in ((taps_one, d1), (taps_two, d2)):
        same = identity()[: weight.shape[0]]
        taps[...] = lax.dot_general(
            weight[...], same, (((0,), (0,)), ((), ())), preferred_element_type=F32
        )


def convolve(terms, planes, rows, g):
    taps = [
        (field[dz, dx : dx + planes, :, 128 * g : 128 * g + 384].reshape(planes * rows, 384),
         weights[dx * 3 + dz, 128 * (1 - g) : 128 * (1 - g) + 384, :])
        for field, weights in terms
        for dx in range(3)
        for dz in range(3)
    ]
    total = None
    for at in range(0, len(taps), 2):
        left = [left for left, _ in taps[at : at + 2]]
        right = [right for _, right in taps[at : at + 2]]
        part = jnp.dot(
            jnp.concatenate(left, axis=1), jnp.concatenate(right, axis=0), preferred_element_type=F32
        )
        total = part if total is None else total + part
    return total.reshape(planes, rows, 256)


def row_mask(rows, start, limit):
    at = lax.broadcasted_iota(jnp.int32, (rows, 512), 0) + start
    return (at >= 0) & (at < limit)


def store_turned(dest, plane, value, keep=slice(None)):
    dest[0, plane] = pltpu.roll(value, 1, 0)[keep].astype(BF)
    dest[1, plane] = value[keep].astype(BF)
    dest[2, plane] = pltpu.roll(value, value.shape[0] - 1, 0)[keep].astype(BF)


def pick_x_kernel(own, out_1, out_2):
    q, _ = position()

    def fill(out, start):
        for p in range(6):
            out[p] = own[(start + p) // 4, :, (start + p) % 4]

    @pl.when(q % 2 == 0)
    def _():
        fill(out_1, 10)
        fill(out_2, 0)

    @pl.when(q % 2 == 1)
    def _():
        fill(out_1, 0)
        fill(out_2, 10)


def pick_z_kernel(own, x1, x2, out_1, out_2):
    _, s = position()

    def fill(out, rows):
        out[0:6] = x1[:, :, rows]
        for x in range(16):
            out[6 + x] = own[x // 4, :, x % 4, rows]
        out[22:28] = x2[:, :, rows]

    @pl.when(s % 2 == 0)
    def _():
        fill(out_1, slice(8, 16))
        fill(out_2, slice(0, 8))

    @pl.when(s % 2 == 1)
    def _():
        fill(out_1, slice(0, 8))
        fill(out_2, slice(8, 16))


def join_kernel(own, x1, x2, out):
    out[0:6] = x1[...]
    out[6:14] = own[...]
    out[14:20] = x2[...]


def x_blocks(own, x1, x2, q):
    plane_1 = 22 * (1 - q % 2)
    blocks = [(pl.ds(plane_1, 6), lambda j: x1[:, j], 0), (pl.ds(22 - plane_1, 6), lambda j: x2[:, j], 22)]
    for i in range(4):
        blocks.append((slice(6 + 4 * i, 10 + 4 * i), lambda j, i=i: own[i, j], 6 + 4 * i))
    return blocks


def own_rows_kernel(own, x1, x2, w1, w2, own_first, own_skip, field, turned, acc):
    q, _ = position()
    for planes, source, _ in x_blocks(own, x1, x2, q):
        for j in range(4):
            field[planes, :, 128 * j : 128 * j + 128] = source(j).astype(F32)

    @pl.loop(0, 28, unroll=4)
    def _(p):
        store_turned(turned, p, field[p])

    for g in range(2):
        acc[:, :, 256 * g : 256 * g + 256] = convolve([(turned, w1)], 26, 16, g)

    @pl.loop(0, 26, unroll=2)
    def _(p):
        x = 16 * q - 5 + p
        value = jnp.where((x >= 0) & (x < 64), jnp.maximum(acc[p], 0.0), 0.0)
        own_first[p] = value.astype(BF)
        store_turned(turned, p, value)

    for g in range(2):
        acc[0:24, :, 256 * g : 256 * g + 256] = convolve([(turned, w2)], 24, 16, g)

    @pl.loop(0, 24, unroll=4)
    def _(p):
        x = 16 * q - 4 + p
        own_skip[p] = jnp.where((x >= 0) & (x < 64), jnp.maximum(acc[p], 0.0), 0.0).astype(BF)


def rim_rows_inside(low, high):
    row = lax.broadcasted_iota(jnp.int32, (16, 512), 0)
    row = jnp.where(row < 8, row + low, row + (high - 8))
    return (row >= 0) & (row < 1024)


def encoder_kernel(
    own, x1, x2, z1, z2, own_first, own_skip, w1, w2, w3, w4,
    skip_out, half_out, half_1, half_2, field, turned, full, acc, half, mid, pooled,
):
    q, s = position()
    x0, z0 = 16 * q, 16 * s
    row_1 = pl.multiple_of(24 * (1 - s % 2), 8)
    row_2 = pl.multiple_of(24 * (s % 2), 8)
    for planes, source, at in x_blocks(own, x1, x2, q):
        for j in range(4):
            lanes = slice(128 * j, 128 * j + 128)
            cells = source(j)
            count = cells.shape[0]
            field[planes, 8:24, lanes] = cells.astype(F32)
            field[planes, pl.ds(row_1, 8), lanes] = z1[at : at + count, j].astype(F32)
            field[planes, pl.ds(row_2, 8), lanes] = z2[at : at + count, j].astype(F32)

    @pl.loop(0, 28, unroll=4)
    def _(p):
        for dz in range(3):
            turned[dz, p] = jnp.concatenate(
                [field[p, pl.ds(dz, 8), :], field[p, pl.ds(22 + dz, 8), :]], axis=0
            ).astype(BF)

    for g in range(2):
        acc[:, :, 256 * g : 256 * g + 256] = convolve([(turned, w1)], 26, 16, g)

    for slot in range(4):
        full[slot, 0:8] = jnp.zeros((8, 512), F32)
        full[slot, 24:32] = jnp.zeros((8, 512), F32)
    inside = rim_rows_inside(z0 - 7, z0 + 15)

    @pl.loop(0, 26, unroll=2)
    def _(p):
        x = x0 - 5 + p
        value = jnp.where(inside & (x >= 0) & (x < 64), jnp.maximum(acc[p], 0.0), 0.0)
        slot = p % 2
        full[slot, 8:24] = own_first[p].astype(F32)
        full[slot, 1:9] = value[0:8]
        full[slot, 23:31] = value[8:16]
        for dz in range(3):
            turned[dz, p] = jnp.concatenate(
                [full[slot, pl.ds(1 + dz, 8), :], full[slot, pl.ds(21 + dz, 8), :]], axis=0
            ).astype(BF)

    for g in range(2):
        acc[0:24, :, 256 * g : 256 * g + 256] = convolve([(turned, w2)], 24, 16, g)

    for slot in range(4):
        full[slot, 0:8] = jnp.zeros((8, 512), F32)
        full[slot, 24:32] = jnp.zeros((8, 512), F32)
    inside_two = rim_rows_inside(z0 - 6, z0 + 14)

    @pl.loop(0, 12, unroll=4)
    def _(h):
        best = None
        for b in range(2):
            p = 2 * h + b
            x = x0 - 4 + p
            rim = jnp.where(inside_two & (x >= 0) & (x < 64), jnp.maximum(acc[p], 0.0), 0.0)
            slot = 2 * (h % 2) + b
            full[slot, 8:24] = own_skip[p].astype(F32)
            full[slot, 2:10] = rim[0:8]
            full[slot, 22:30] = rim[8:16]
            value = full[slot]
            store_turned(skip_out, jnp.where((p >= 3) & (p < 21), p - 3, 18), value, slice(8, 24))
            best = value if best is None else jnp.maximum(best, value)
        best = jnp.maximum(best, pltpu.roll(best, 480, 1))
        pieces = []
        for t in range(4):
            pooled[h % 4, t] = best[:, 128 * t : 128 * t + 128]
            pieces.append(
                jnp.maximum(
                    pooled[h % 4, t, pl.ds(0, 16, stride=2), :], pooled[h % 4, t, pl.ds(1, 16, stride=2), :]
                )
            )
        store_turned(half, h, jnp.concatenate(pieces, axis=1))

    for g in range(2):
        acc[0:10, 0:16, 256 * g : 256 * g + 256] = convolve([(half, w3)], 10, 16, g)

    @pl.loop(0, 10, unroll=5)
    def _(p):
        x = 8 * q - 1 + p
        inside = row_mask(16, 8 * s - 4, 512) & (x >= 0) & (x < 32)
        store_turned(mid, p, jnp.where(inside, jnp.maximum(acc[p, 0:16], 0.0), 0.0))

    for g in range(2):
        acc[0:8, 0:16, 256 * g : 256 * g + 256] = convolve([(mid, w4)], 8, 16, g)
    half_out[...] = jnp.maximum(acc[0:8, 4:12, :], 0.0).astype(BF)

    @pl.when(q % 2 == 0)
    def _():
        half_1[...] = half_out[2:8]
        half_2[...] = half_out[0:6]

    @pl.when(q % 2 == 1)
    def _():
        half_1[...] = half_out[0:6]
        half_2[...] = half_out[2:8]


def skip_kernel(skip, w6s, out):
    for g in range(2):
        out[:, :, 256 * g : 256 * g + 256] = convolve([(skip.at[:, 0:18], w6s)], 16, 16, g)


def depthwise(source, taps, planes, offset, shifted):
    for dz in range(3):
        shifted[dz, 0 : planes + 2] = source[0 : planes + 2, pl.ds(offset + dz, 8), :]
    sums = []
    for t in range(4):
        total = jnp.zeros((planes, 8, 128), F32)
        for dx in range(3):
            for dy in range(3):
                at = t + dy - 1
                if not 0 <= at < 4:
                    continue
                for dz in range(3):
                    tap = (dx * 3 + dy) * 3 + dz
                    factor = taps[tap : tap + 1, :].reshape(1, 1, 128)
                    total += shifted[dz, dx : dx + planes, :, 128 * at : 128 * at + 128] * factor
        sums.append(total.reshape(planes * 8, 128).astype(BF))
    return sums


def decoder_kernel(
    own, x1, x2, z1, z2, skip_part, d1, p1, d2, p2, w5u, w5s, w6u,
    out, whole, sides, pooled, quarter, mixed, grown, ups, acc, tall, fine, shifted,
):
    q, s = position()
    plane_1 = 14 * (1 - q % 2)
    plane_2 = 14 - plane_1
    row_1 = pl.multiple_of(16 * (1 - s % 2), 8)
    row_2 = pl.multiple_of(16 * (s % 2), 8)
    for start, size, source, at in ((plane_1, 6, x1, 0), (6, 8, own, 6), (plane_2, 6, x2, 14)):
        whole[pl.ds(start, size), 8:16, :] = source[...].astype(F32)
        whole[pl.ds(start, size), pl.ds(row_1, 8), :] = z1[at : at + size].astype(F32)
        whole[pl.ds(start, size), pl.ds(row_2, 8), :] = z2[at : at + size].astype(F32)

    @pl.loop(0, 12, unroll=4)
    def _(p):
        for dz in range(3):
            sides[dz, p] = whole[p + 4, pl.ds(3 + dz, 16), :].astype(BF)

    quarter[...] = jnp.zeros_like(quarter)

    @pl.loop(0, 10, unroll=5)
    def _(p):
        best = jnp.maximum(whole[2 * p], whole[2 * p + 1])
        best = jnp.maximum(best, pltpu.roll(best, 448, 1))
        for t in range(4):
            pooled[0:24, :] = best[:, 128 * t : 128 * t + 128]
            quarter[p, 0:12, 128 * t : 128 * t + 128] = jnp.maximum(
                pooled[pl.ds(0, 12, stride=2), :], pooled[pl.ds(1, 12, stride=2), :]
            )

    mixed[...] = jnp.zeros_like(mixed)
    spread = depthwise(quarter, d1, 8, 1, shifted)
    plane = lax.broadcasted_iota(jnp.int32, (8, 8, 128), 0) + (4 * q - 2)
    row = lax.broadcasted_iota(jnp.int32, (8, 8, 128), 1) + (4 * s - 2)
    inside = (plane >= 0) & (plane < 16) & (row >= 0) & (row < 256)
    for t in range(4):
        value = lax.dot_general(
            spread[t][:, :64], p1[...], (((1,), (1,)), ((), ())), preferred_element_type=F32
        ).reshape(8, 8, 128)
        value = jnp.where(inside, jnp.maximum(value, 0.0), 0.0)
        mixed[:, 0:8, 128 * t : 128 * t + 128] = value.astype(BF).astype(F32)

    spread = depthwise(mixed, d2, 6, 0, shifted)
    plane = lax.broadcasted_iota(jnp.int32, (6, 8, 128), 0) + (4 * q - 1)
    row = lax.broadcasted_iota(jnp.int32, (6, 8, 128), 1) + (4 * s - 1)
    inside = (plane >= 0) & (plane < 16) & (row >= 0) & (row < 256)
    grown[...] = jnp.zeros_like(grown)
    for t in range(4):
        value = lax.dot_general(
            spread[t], p2[...], (((1,), (1,)), ((), ())), preferred_element_type=F32
        ).reshape(6, 8, 128)
        value = jnp.where(inside, jnp.maximum(value, 0.0), 0.0)
        for p in range(6):
            grown[pl.ds(8, 8, stride=2), :] = value[p]
            grown[pl.ds(9, 8, stride=2), :] = value[p]
            for dz in range(3):
                rows = grown[pl.ds(5 + dz, 16), :].astype(BF)
                ups[dz, 2 * p, :, 128 * t : 128 * t + 128] = rows
                ups[dz, 2 * p + 1, :, 128 * t : 128 * t + 128] = rows

    for g in range(2):
        acc[0:10, :, 256 * g : 256 * g + 256] = convolve(
            [(ups, w5u), (sides, w5s)], 10, 16, g
        )

    @pl.loop(0, 10, unroll=5)
    def _(p):
        x = 8 * q - 1 + p
        inside = row_mask(16, 8 * s - 4, 512) & (x >= 0) & (x < 32)
        value = jnp.where(inside, jnp.maximum(acc[p], 0.0), 0.0)
        for t in range(4):
            tall[t, pl.ds(0, 16, stride=2), :] = value[:, 128 * t : 128 * t + 128]
            tall[t, pl.ds(1, 16, stride=2), :] = value[:, 128 * t : 128 * t + 128]
        for dz in range(3):
            rows = jnp.concatenate([tall[t, pl.ds(7 + dz, 16), :] for t in range(4)], axis=1).astype(BF)
            fine[dz, 2 * p] = rows
            fine[dz, 2 * p + 1] = rows

    for g in range(2):
        total = convolve([(fine.at[:, 1:19], w6u)], 16, 16, g)
        total = (total + skip_part[:, :, 256 * g : 256 * g + 256]).astype(BF)
        for i in range(4):
            for j in range(2):
                out[i, 2 * g + j] = total[4 * i : 4 * i + 4, :, 128 * j : 128 * j + 128]


def call(kernel, outs, scratch=(), flops=0, limit=8):
    whole = pl.BlockSpec(memory_space=pltpu.VMEM)

    def run(*args):
        return pl.pallas_call(
            kernel,
            out_shape=outs,
            in_specs=[whole] * len(args),
            out_specs=jax.tree.map(lambda _: whole, outs),
            scratch_shapes=list(scratch),
            compiler_params=pltpu.CompilerParams(vmem_limit_bytes=limit << 20),
            cost_estimate=pl.CostEstimate(flops=flops, bytes_accessed=4 << 20, transcendentals=0),
        )(*args)

    return run


def shape(*dims):
    return jax.ShapeDtypeStruct(dims, BF)


def forward(
    features, conv_one, conv_two, conv_three, conv_four, depth_one, point_one, depth_two, point_two,
    conv_five, conv_six,
):
    bands = shape(9, 512, 256)

    rows = call(to_rows_kernel, shape(16, 4, 16, 128))(features)
    own = lax.all_to_all(rows, PLANE, 0, 0, tiled=True, axis_index_groups=GROUPS)
    own = own.reshape(4, 4, 4, 16, 128)
    w1, w2, w3, w4 = call(encoder_weights_kernel, (bands,) * 4, limit=LIMITS[0])(
        conv_one, conv_two, conv_three, conv_four
    )
    taps = jax.ShapeDtypeStruct((27, 128), F32)
    w5u, w5s, w6u, w6s, taps_one, taps_two = call(
        decoder_weights_kernel, (bands,) * 4 + (taps,) * 2, limit=LIMITS[1]
    )(conv_five, conv_six, depth_one, depth_two)
    x_swaps = [swap_pairs(1, 0, parity) for parity in range(2)]
    z_swaps = [swap_pairs(0, 1, parity) for parity in range(2)]
    pieces = call(pick_x_kernel, (shape(6, 4, 16, 128),) * 2, flops=8 << 30)(own)
    x_got = [lax.ppermute(piece, EVERY, pairs) for piece, pairs in zip(pieces, x_swaps)]
    pieces = call(pick_z_kernel, (shape(28, 4, 8, 128),) * 2)(own, *x_got)
    z_got = []
    for turn in range(2):
        z_got.append(lax.ppermute(pieces[turn], EVERY, z_swaps[turn]))
    own_first, own_skip = call(
        own_rows_kernel,
        (shape(26, 16, 512), shape(24, 16, 512)),
        [
            pltpu.VMEM((28, 16, 512), F32),
            pltpu.VMEM((3, 28, 16, 512), BF),
            pltpu.VMEM((26, 16, 512), F32),
        ],
        flops=3 << 30,
        limit=16,
    )(own, *x_got, w1, w2)
    skip, half_skip, *pieces = call(
        encoder_kernel,
        (shape(3, 19, 16, 512), shape(8, 8, 512), shape(6, 8, 512), shape(6, 8, 512)),
        [
            pltpu.VMEM((28, 32, 512), F32),
            pltpu.VMEM((3, 28, 16, 512), BF),
            pltpu.VMEM((4, 32, 512), F32),
            pltpu.VMEM((26, 16, 512), F32),
            pltpu.VMEM((3, 12, 16, 512), BF),
            pltpu.VMEM((3, 10, 16, 512), BF),
            pltpu.VMEM((4, 4, 32, 128), F32),
        ],
        flops=6 << 30,
        limit=LIMITS[2],
    )(own, *x_got, *z_got, own_first, own_skip, w1, w2, w3, w4)
    x_got = []
    for turn in range(2):
        x_got.append(lax.ppermute(pieces[turn], EVERY, x_swaps[turn]))
    broad = call(join_kernel, shape(20, 8, 512))(half_skip, *x_got)
    z_got = []
    for turn in range(2):
        z_got.append(lax.ppermute(broad, EVERY, z_swaps[turn]))
    skip_part = call(
        skip_kernel, jax.ShapeDtypeStruct((16, 16, 512), F32), flops=2 << 30, limit=12
    )(skip, w6s)
    rows = call(
        decoder_kernel,
        shape(4, 4, 4, 16, 128),
        [
            pltpu.VMEM((20, 24, 512), F32),
            pltpu.VMEM((3, 12, 16, 512), BF),
            pltpu.VMEM((32, 128), F32),
            pltpu.VMEM((10, 16, 512), F32),
            pltpu.VMEM((8, 16, 512), F32),
            pltpu.VMEM((32, 128), F32),
            pltpu.VMEM((3, 12, 16, 512), BF),
            pltpu.VMEM((16, 16, 512), F32),
            pltpu.VMEM((4, 32, 128), F32),
            pltpu.VMEM((3, 20, 16, 512), BF),
            pltpu.VMEM((3, 10, 8, 512), F32),
        ],
        flops=2 << 30,
        limit=LIMITS[3],
    )(
        half_skip, *x_got, *z_got, skip_part,
        taps_one, point_one, taps_two, point_two, w5u, w5s, w6u,
    )
    back = lax.all_to_all(
        rows.reshape(16, 4, 16, 128), PLANE, 0, 0, tiled=True, axis_index_groups=GROUPS
    )
    return call(from_rows_kernel, shape(32, 4, 4, 256))(back)


def solution(mesh):
    in_specs = (P(None, "gx", "gy", "gz"), P(), P(), P(), P(), P(), P(), P(), P(), P(), P())
    out_specs = P(None, "gx", "gy", "gz")
    return jax.shard_map(forward, mesh=mesh, in_specs=in_specs, out_specs=out_specs, check_vma=False)
```

```python
import jax
import jax.numpy as jnp
from jax import lax
from jax.experimental import pallas as pl
from jax.experimental.pallas import tpu as pltpu
from jax.sharding import PartitionSpec as P


BF = jnp.bfloat16
F32 = jnp.float32
PLANE = ("gx", "gy")
EVERY = ("gx", "gy", "gz")
LIMITS = (8, 8, 12, 14)


def slab_at(z_low, across, core):
    step = across + z_low * (3 - 2 * across)
    return 8 * z_low + 2 * step + (core + step) % 2


SLABS = [slab_at(rank // 8, rank % 4, rank // 4 % 2) for rank in range(16)]


def device_at(q, slab, k):
    rank = SLABS.index(slab)
    return ((q * 4 + rank // 4) * 4 + rank % 4) * 4 + k


def swap_pairs(step_x, step_z, parity):
    pairs = []
    for q in range(4):
        for s in range(64):
            to_q, to_s = q + step_x, s + step_z
            if (q * step_x + s * step_z) % 2 == parity and to_q < 4 and to_s < 64:
                here = device_at(q, s % 16, s // 16)
                there = device_at(to_q, to_s % 16, to_s // 16)
                pairs += [(here, there), (there, here)]
    return pairs


GROUPS = [list(range(16 * q, 16 * q + 16)) for q in range(4)]


def position():
    gx, gy, gz = lax.axis_index("gx"), lax.axis_index("gy"), lax.axis_index("gz")
    return gx // 4, gz * 16 + slab_at(gx // 2 % 2, gy, gx % 2)


def identity():
    row = lax.broadcasted_iota(jnp.int32, (128, 128), 0)
    lane = lax.broadcasted_iota(jnp.int32, (128, 128), 1)
    return jnp.where(row == lane, 1.0, 0.0).astype(BF)


def to_rows_kernel(cells_ref, out_ref):
    same = identity()
    for x in range(4):
        cells = jnp.concatenate([cells_ref[:, x, y, :] for y in range(4)], axis=0)
        turned = lax.dot_general(
            cells, same, (((0,), (0,)), ((), ())), preferred_element_type=F32
        ).astype(BF)
        for rank, slab in enumerate(SLABS):
            out_ref[rank, x] = turned[16 * slab : 16 * slab + 16]


def from_rows_kernel(rows_ref, out_ref):
    same = identity()
    for x in range(4):
        rows = jnp.concatenate([rows_ref[SLABS.index(slab), x] for slab in range(16)], axis=0)
        turned = lax.dot_general(
            same, rows, (((1,), (1,)), ((), ())), preferred_element_type=F32
        ).astype(BF)
        for y in range(4):
            out_ref[:, x, y, :] = turned[32 * y : 32 * y + 32]


def band(spread, out_ref, stride, first, used, lanes_in, lanes_out, grown=False):
    per_tile = 128 // lanes_out
    lead = 128 // lanes_in
    group = lax.broadcasted_iota(jnp.int32, (used, 128), 1) // lanes_out
    chosen = [jnp.where(group == j, 1.0, 0.0).astype(BF) for j in range(per_tile)]
    empty = jnp.zeros((lanes_in, 128), BF)
    for dx in range(3):
        for dz in range(3):
            tap = dx * 3 + dz
            parts = []
            for dy in range(3):
                start = ((dx * 3 + dy) * 3 + dz) * stride + first
                parts.append(spread[start : start + used, :])
            if grown:
                pieces = {-1: parts[2], 0: parts[1] + parts[2], 1: parts[0] + parts[1], 2: parts[0]}
            else:
                pieces = {1: parts[0], 0: parts[1], -1: parts[2]}
            pieces = {gap: piece.astype(BF) for gap, piece in pieces.items()}
            made = {}
            for at in range(out_ref.shape[1] // lanes_in):
                for tile in range(2):
                    key = (2 if grown else 1) * (at - lead) - per_tile * tile
                    if key not in made:
                        block = None
                        for gap, piece in pieces.items():
                            if 0 <= key + gap < per_tile:
                                term = piece * chosen[key + gap]
                                block = term if block is None else block + term
                        made[key] = block
                    block = made[key]
                    lanes = slice(128 * tile, 128 * tile + 128)
                    if block is None:
                        out_ref[tap, at * lanes_in : (at + 1) * lanes_in, lanes] = empty
                    else:
                        out_ref[tap, at * lanes_in : at * lanes_in + used, lanes] = block
                        if used < lanes_in:
                            out_ref[tap, at * lanes_in + used : (at + 1) * lanes_in, lanes] = empty[
                                : lanes_in - used
                            ]


def spread_lanes(weight, lanes_out):
    outs = weight.shape[0]
    row = lax.broadcasted_iota(jnp.int32, (outs, 128), 0)
    lane = lax.broadcasted_iota(jnp.int32, (outs, 128), 1)
    chosen = jnp.where(lane % lanes_out == row, 1.0, 0.0).astype(BF)
    return lax.dot_general(weight, chosen, (((0,), (0,)), ((), ())), preferred_element_type=F32)


def encoder_weights_kernel(w1, w2, w3, w4, o1, o2, o3, o4):
    band(spread_lanes(w1[...], 32), o1, 32, 0, 32, 32, 32)
    band(spread_lanes(w2[...], 32), o2, 32, 0, 32, 32, 32)
    band(spread_lanes(w3[...], 64), o3, 32, 0, 32, 64, 64)
    band(spread_lanes(w4[...], 64), o4, 64, 0, 64, 64, 64)


def fine_weights_kernel(w6, o6u, o6s):
    fine = spread_lanes(w6[...], 32)
    band(fine, o6u, 96, 0, 64, 64, 32, grown=True)
    band(fine, o6s, 96, 64, 32, 32, 32)


def half_weights_kernel(w5, d1, d2, o5u, o5s, taps_one, taps_two):
    wide = spread_lanes(w5[...], 64)
    band(wide, o5u, 192, 0, 128, 128, 64, grown=True)
    band(wide, o5s, 192, 128, 64, 64, 64)
    for taps, weight in ((taps_one, d1), (taps_two, d2)):
        same = identity()[: weight.shape[1]]
        taps[...] = jnp.dot(weight[...], same, preferred_element_type=F32)


def convolve(terms, planes, rows, g):
    taps = [
        (field[dz, dx : dx + planes, :, 128 * g : 128 * g + 384].reshape(planes * rows, 384),
         weights[dx * 3 + dz, 128 * (1 - g) : 128 * (1 - g) + 384, :])
        for field, weights in terms
        for dx in range(3)
        for dz in range(3)
    ]
    total = None
    for at in range(0, len(taps), 2):
        left = [left for left, _ in taps[at : at + 2]]
        right = [right for _, right in taps[at : at + 2]]
        part = jnp.dot(
            jnp.concatenate(left, axis=1), jnp.concatenate(right, axis=0), preferred_element_type=F32
        )
        total = part if total is None else total + part
    return total.reshape(planes, rows, 256)


def row_mask(rows, start, limit):
    at = lax.broadcasted_iota(jnp.int32, (rows, 512), 0) + start
    return (at >= 0) & (at < limit)


def store_turned(dest, plane, value, keep=slice(None)):
    dest[0, plane] = pltpu.roll(value, 1, 0)[keep].astype(BF)
    dest[1, plane] = value[keep].astype(BF)
    dest[2, plane] = pltpu.roll(value, value.shape[0] - 1, 0)[keep].astype(BF)


def pick_x_kernel(own, out_1, out_2):
    q, _ = position()

    def fill(out, start):
        for p in range(6):
            out[p] = own[(start + p) // 4, :, (start + p) % 4]

    @pl.when(q % 2 == 0)
    def _():
        fill(out_1, 10)
        fill(out_2, 0)

    @pl.when(q % 2 == 1)
    def _():
        fill(out_1, 0)
        fill(out_2, 10)


def pick_z_kernel(own, x1, x2, out_1, out_2):
    _, s = position()

    def fill(out, rows):
        out[0:6] = x1[:, :, rows]
        for x in range(16):
            out[6 + x] = own[x // 4, :, x % 4, rows]
        out[22:28] = x2[:, :, rows]

    @pl.when(s % 2 == 0)
    def _():
        fill(out_1, slice(8, 16))
        fill(out_2, slice(0, 8))

    @pl.when(s % 2 == 1)
    def _():
        fill(out_1, slice(0, 8))
        fill(out_2, slice(8, 16))


def join_kernel(own, x1, x2, out):
    out[0:6] = x1[...]
    out[6:14] = own[...]
    out[14:20] = x2[...]


def x_blocks(own, x1, x2, q):
    plane_1 = 22 * (1 - q % 2)
    blocks = [(pl.ds(plane_1, 6), lambda j: x1[:, j], 0), (pl.ds(22 - plane_1, 6), lambda j: x2[:, j], 22)]
    for i in range(4):
        blocks.append((slice(6 + 4 * i, 10 + 4 * i), lambda j, i=i: own[i, j], 6 + 4 * i))
    return blocks


def own_rows_kernel(own, x1, x2, w1, w2, own_first, own_skip, field, turned, acc):
    q, _ = position()
    for planes, source, _ in x_blocks(own, x1, x2, q):
        for j in range(4):
            field[planes, :, 128 * j : 128 * j + 128] = source(j).astype(F32)

    @pl.loop(0, 28, unroll=4)
    def _(p):
        store_turned(turned, p, field[p])

    for g in range(2):
        acc[:, :, 256 * g : 256 * g + 256] = convolve([(turned, w1)], 26, 16, g)

    @pl.loop(0, 26, unroll=2)
    def _(p):
        x = 16 * q - 5 + p
        value = jnp.where((x >= 0) & (x < 64), jnp.maximum(acc[p], 0.0), 0.0)
        own_first[p] = value.astype(BF)
        store_turned(turned, p, value)

    for g in range(2):
        acc[0:24, :, 256 * g : 256 * g + 256] = convolve([(turned, w2)], 24, 16, g)

    @pl.loop(0, 24, unroll=4)
    def _(p):
        x = 16 * q - 4 + p
        own_skip[p] = jnp.where((x >= 0) & (x < 64), jnp.maximum(acc[p], 0.0), 0.0).astype(BF)


def rim_rows_inside(low, high):
    row = lax.broadcasted_iota(jnp.int32, (16, 512), 0)
    row = jnp.where(row < 8, row + low, row + (high - 8))
    return (row >= 0) & (row < 1024)


def encoder_kernel(
    own, x1, x2, z1, z2, own_first, own_skip, w1, w2, w3, w4,
    skip_out, half_out, half_1, half_2, field, turned, full, acc, half, mid, pooled,
):
    q, s = position()
    x0, z0 = 16 * q, 16 * s
    row_1 = pl.multiple_of(24 * (1 - s % 2), 8)
    row_2 = pl.multiple_of(24 * (s % 2), 8)
    for planes, source, at in x_blocks(own, x1, x2, q):
        for j in range(4):
            lanes = slice(128 * j, 128 * j + 128)
            cells = source(j)
            count = cells.shape[0]
            field[planes, 8:24, lanes] = cells.astype(F32)
            field[planes, pl.ds(row_1, 8), lanes] = z1[at : at + count, j].astype(F32)
            field[planes, pl.ds(row_2, 8), lanes] = z2[at : at + count, j].astype(F32)

    @pl.loop(0, 28, unroll=4)
    def _(p):
        for dz in range(3):
            turned[dz, p] = jnp.concatenate(
                [field[p, pl.ds(dz, 8), :], field[p, pl.ds(22 + dz, 8), :]], axis=0
            ).astype(BF)

    for g in range(2):
        acc[:, :, 256 * g : 256 * g + 256] = convolve([(turned, w1)], 26, 16, g)

    for slot in range(4):
        full[slot, 0:8] = jnp.zeros((8, 512), F32)
        full[slot, 24:32] = jnp.zeros((8, 512), F32)
    inside = rim_rows_inside(z0 - 7, z0 + 15)

    @pl.loop(0, 26, unroll=2)
    def _(p):
        x = x0 - 5 + p
        value = jnp.where(inside & (x >= 0) & (x < 64), jnp.maximum(acc[p], 0.0), 0.0)
        slot = p % 2
        full[slot, 8:24] = own_first[p].astype(F32)
        full[slot, 1:9] = value[0:8]
        full[slot, 23:31] = value[8:16]
        for dz in range(3):
            turned[dz, p] = jnp.concatenate(
                [full[slot, pl.ds(1 + dz, 8), :], full[slot, pl.ds(21 + dz, 8), :]], axis=0
            ).astype(BF)

    for g in range(2):
        acc[0:24, :, 256 * g : 256 * g + 256] = convolve([(turned, w2)], 24, 16, g)

    for slot in range(4):
        full[slot, 0:8] = jnp.zeros((8, 512), F32)
        full[slot, 24:32] = jnp.zeros((8, 512), F32)
    inside_two = rim_rows_inside(z0 - 6, z0 + 14)

    @pl.loop(0, 12, unroll=4)
    def _(h):
        best = None
        for b in range(2):
            p = 2 * h + b
            x = x0 - 4 + p
            rim = jnp.where(inside_two & (x >= 0) & (x < 64), jnp.maximum(acc[p], 0.0), 0.0)
            slot = 2 * (h % 2) + b
            full[slot, 8:24] = own_skip[p].astype(F32)
            full[slot, 2:10] = rim[0:8]
            full[slot, 22:30] = rim[8:16]
            value = full[slot]
            store_turned(skip_out, jnp.where((p >= 3) & (p < 21), p - 3, 18), value, slice(8, 24))
            best = value if best is None else jnp.maximum(best, value)
        best = jnp.maximum(best, pltpu.roll(best, 480, 1))
        pieces = []
        for t in range(4):
            pooled[h % 4, t] = best[:, 128 * t : 128 * t + 128]
            pieces.append(
                jnp.maximum(
                    pooled[h % 4, t, pl.ds(0, 16, stride=2), :], pooled[h % 4, t, pl.ds(1, 16, stride=2), :]
                )
            )
        store_turned(half, h, jnp.concatenate(pieces, axis=1))

    for g in range(2):
        acc[0:10, 0:16, 256 * g : 256 * g + 256] = convolve([(half, w3)], 10, 16, g)

    @pl.loop(0, 10, unroll=5)
    def _(p):
        x = 8 * q - 1 + p
        inside = row_mask(16, 8 * s - 4, 512) & (x >= 0) & (x < 32)
        store_turned(mid, p, jnp.where(inside, jnp.maximum(acc[p, 0:16], 0.0), 0.0))

    for g in range(2):
        acc[0:8, 0:16, 256 * g : 256 * g + 256] = convolve([(mid, w4)], 8, 16, g)
    half_out[...] = jnp.maximum(acc[0:8, 4:12, :], 0.0).astype(BF)

    @pl.when(q % 2 == 0)
    def _():
        half_1[...] = half_out[2:8]
        half_2[...] = half_out[0:6]

    @pl.when(q % 2 == 1)
    def _():
        half_1[...] = half_out[0:6]
        half_2[...] = half_out[2:8]


def skip_kernel(skip, w6s, out):
    for g in range(2):
        out[:, :, 256 * g : 256 * g + 256] = convolve([(skip.at[:, 0:18], w6s)], 16, 16, g)


def depthwise(source, taps, planes, offset, shifted):
    for dz in range(3):
        shifted[dz, 0 : planes + 2] = source[0 : planes + 2, pl.ds(offset + dz, 8), :]
    sums = []
    for t in range(4):
        total = jnp.zeros((planes, 8, 128), F32)
        for dx in range(3):
            for dy in range(3):
                at = t + dy - 1
                if not 0 <= at < 4:
                    continue
                for dz in range(3):
                    tap = (dx * 3 + dy) * 3 + dz
                    factor = taps[tap : tap + 1, :].reshape(1, 1, 128)
                    total += shifted[dz, dx : dx + planes, :, 128 * at : 128 * at + 128] * factor
        sums.append(total.reshape(planes * 8, 128).astype(BF))
    return sums


def decoder_kernel(
    own, x1, x2, z1, z2, skip_part, d1, p1, d2, p2, w5u, w5s, w6u,
    out, whole, sides, pooled, quarter, mixed, grown, ups, acc, tall, fine, shifted,
):
    q, s = position()
    plane_1 = 14 * (1 - q % 2)
    plane_2 = 14 - plane_1
    row_1 = pl.multiple_of(16 * (1 - s % 2), 8)
    row_2 = pl.multiple_of(16 * (s % 2), 8)
    for start, size, source, at in ((plane_1, 6, x1, 0), (6, 8, own, 6), (plane_2, 6, x2, 14)):
        whole[pl.ds(start, size), 8:16, :] = source[...].astype(F32)
        whole[pl.ds(start, size), pl.ds(row_1, 8), :] = z1[at : at + size].astype(F32)
        whole[pl.ds(start, size), pl.ds(row_2, 8), :] = z2[at : at + size].astype(F32)

    @pl.loop(0, 12, unroll=4)
    def _(p):
        for dz in range(3):
            sides[dz, p] = whole[p + 4, pl.ds(3 + dz, 16), :].astype(BF)

    quarter[...] = jnp.zeros_like(quarter)

    @pl.loop(0, 10, unroll=5)
    def _(p):
        best = jnp.maximum(whole[2 * p], whole[2 * p + 1])
        best = jnp.maximum(best, pltpu.roll(best, 448, 1))
        for t in range(4):
            pooled[0:24, :] = best[:, 128 * t : 128 * t + 128]
            quarter[p, 0:12, 128 * t : 128 * t + 128] = jnp.maximum(
                pooled[pl.ds(0, 12, stride=2), :], pooled[pl.ds(1, 12, stride=2), :]
            )

    mixed[...] = jnp.zeros_like(mixed)
    spread = depthwise(quarter, d1, 8, 1, shifted)
    plane = lax.broadcasted_iota(jnp.int32, (8, 8, 128), 0) + (4 * q - 2)
    row = lax.broadcasted_iota(jnp.int32, (8, 8, 128), 1) + (4 * s - 2)
    inside = (plane >= 0) & (plane < 16) & (row >= 0) & (row < 256)
    for t in range(4):
        value = jnp.dot(spread[t][:, :64], p1[...], preferred_element_type=F32).reshape(8, 8, 128)
        value = jnp.where(inside, jnp.maximum(value, 0.0), 0.0)
        mixed[:, 0:8, 128 * t : 128 * t + 128] = value.astype(BF).astype(F32)

    spread = depthwise(mixed, d2, 6, 0, shifted)
    plane = lax.broadcasted_iota(jnp.int32, (6, 8, 128), 0) + (4 * q - 1)
    row = lax.broadcasted_iota(jnp.int32, (6, 8, 128), 1) + (4 * s - 1)
    inside = (plane >= 0) & (plane < 16) & (row >= 0) & (row < 256)
    grown[...] = jnp.zeros_like(grown)
    for t in range(4):
        value = lax.dot_general(
            spread[t], p2[...], (((1,), (1,)), ((), ())), preferred_element_type=F32
        ).reshape(6, 8, 128)
        value = jnp.where(inside, jnp.maximum(value, 0.0), 0.0)
        for p in range(6):
            grown[pl.ds(8, 8, stride=2), :] = value[p]
            grown[pl.ds(9, 8, stride=2), :] = value[p]
            for dz in range(3):
                rows = grown[pl.ds(5 + dz, 16), :].astype(BF)
                ups[dz, 2 * p, :, 128 * t : 128 * t + 128] = rows
                ups[dz, 2 * p + 1, :, 128 * t : 128 * t + 128] = rows

    for g in range(2):
        acc[0:10, :, 256 * g : 256 * g + 256] = convolve(
            [(ups, w5u), (sides, w5s)], 10, 16, g
        )

    @pl.loop(0, 10, unroll=5)
    def _(p):
        x = 8 * q - 1 + p
        inside = row_mask(16, 8 * s - 4, 512) & (x >= 0) & (x < 32)
        value = jnp.where(inside, jnp.maximum(acc[p], 0.0), 0.0)
        for t in range(4):
            tall[t, pl.ds(0, 16, stride=2), :] = value[:, 128 * t : 128 * t + 128]
            tall[t, pl.ds(1, 16, stride=2), :] = value[:, 128 * t : 128 * t + 128]
        for dz in range(3):
            rows = jnp.concatenate([tall[t, pl.ds(7 + dz, 16), :] for t in range(4)], axis=1).astype(BF)
            fine[dz, 2 * p] = rows
            fine[dz, 2 * p + 1] = rows

    for g in range(2):
        total = convolve([(fine.at[:, 1:19], w6u)], 16, 16, g)
        total = (total + skip_part[:, :, 256 * g : 256 * g + 256]).astype(BF)
        for i in range(4):
            for j in range(2):
                out[i, 2 * g + j] = total[4 * i : 4 * i + 4, :, 128 * j : 128 * j + 128]


def call(kernel, outs, scratch=(), flops=0, limit=8):
    whole = pl.BlockSpec(memory_space=pltpu.VMEM)

    def run(*args):
        return pl.pallas_call(
            kernel,
            out_shape=outs,
            in_specs=[whole] * len(args),
            out_specs=jax.tree.map(lambda _: whole, outs),
            scratch_shapes=list(scratch),
            compiler_params=pltpu.CompilerParams(vmem_limit_bytes=limit << 20),
            cost_estimate=pl.CostEstimate(flops=flops, bytes_accessed=4 << 20, transcendentals=0),
        )(*args)

    return run


def shape(*dims):
    return jax.ShapeDtypeStruct(dims, BF)


def forward(
    features, conv_one, conv_two, conv_three, conv_four, depth_one, point_one, depth_two, point_two,
    conv_five, conv_six,
):
    bands = shape(9, 512, 256)

    rows = call(to_rows_kernel, shape(16, 4, 16, 128))(features)
    own = lax.all_to_all(rows, PLANE, 0, 0, tiled=True, axis_index_groups=GROUPS)
    own = own.reshape(4, 4, 4, 16, 128)
    w1, w2, w3, w4 = call(encoder_weights_kernel, (bands,) * 4, limit=LIMITS[0])(
        conv_one, conv_two, conv_three, conv_four
    )
    w6u, w6s = call(fine_weights_kernel, (bands,) * 2, limit=8)(conv_six)
    taps = jax.ShapeDtypeStruct((27, 128), F32)
    w5u, w5s, taps_one, taps_two = call(
        half_weights_kernel, (bands,) * 2 + (taps,) * 2, limit=8
    )(conv_five, depth_one.T, depth_two.T)
    x_swaps = [swap_pairs(1, 0, parity) for parity in range(2)]
    z_swaps = [swap_pairs(0, 1, parity) for parity in range(2)]
    pieces = call(pick_x_kernel, (shape(6, 4, 16, 128),) * 2, flops=8 << 30)(own)
    x_got = []
    for turn in range(2):
        x_got.append(lax.ppermute(pieces[turn], EVERY, x_swaps[turn]))
    pieces = call(pick_z_kernel, (shape(28, 4, 8, 128),) * 2)(own, *x_got)
    z_got = []
    for turn in range(2):
        z_got.append(lax.ppermute(pieces[turn], EVERY, z_swaps[turn]))
    own_first, own_skip = call(
        own_rows_kernel,
        (shape(26, 16, 512), shape(24, 16, 512)),
        [
            pltpu.VMEM((28, 16, 512), F32),
            pltpu.VMEM((3, 28, 16, 512), BF),
            pltpu.VMEM((26, 16, 512), F32),
        ],
        flops=3 << 30,
        limit=16,
    )(own, *x_got, w1, w2)
    skip, half_skip, *pieces = call(
        encoder_kernel,
        (shape(3, 19, 16, 512), shape(8, 8, 512), shape(6, 8, 512), shape(6, 8, 512)),
        [
            pltpu.VMEM((28, 32, 512), F32),
            pltpu.VMEM((3, 28, 16, 512), BF),
            pltpu.VMEM((4, 32, 512), F32),
            pltpu.VMEM((26, 16, 512), F32),
            pltpu.VMEM((3, 12, 16, 512), BF),
            pltpu.VMEM((3, 10, 16, 512), BF),
            pltpu.VMEM((4, 4, 32, 128), F32),
        ],
        flops=6 << 30,
        limit=LIMITS[2],
    )(own, *x_got, *z_got, own_first, own_skip, w1, w2, w3, w4)
    x_got = []
    for turn in range(2):
        x_got.append(lax.ppermute(pieces[turn], EVERY, x_swaps[turn]))
    broad = call(join_kernel, shape(20, 8, 512))(half_skip, *x_got)
    z_got = []
    for turn in range(2):
        z_got.append(lax.ppermute(broad, EVERY, z_swaps[turn]))
    skip_part = call(
        skip_kernel, jax.ShapeDtypeStruct((16, 16, 512), F32), flops=2 << 30, limit=12
    )(skip, w6s)
    rows = call(
        decoder_kernel,
        shape(4, 4, 4, 16, 128),
        [
            pltpu.VMEM((20, 24, 512), F32),
            pltpu.VMEM((3, 12, 16, 512), BF),
            pltpu.VMEM((32, 128), F32),
            pltpu.VMEM((10, 16, 512), F32),
            pltpu.VMEM((8, 16, 512), F32),
            pltpu.VMEM((32, 128), F32),
            pltpu.VMEM((3, 12, 16, 512), BF),
            pltpu.VMEM((16, 16, 512), F32),
            pltpu.VMEM((4, 32, 128), F32),
            pltpu.VMEM((3, 20, 16, 512), BF),
            pltpu.VMEM((3, 10, 8, 512), F32),
        ],
        flops=2 << 30,
        limit=LIMITS[3],
    )(
        half_skip, *x_got, *z_got, skip_part,
        taps_one, point_one.T, taps_two, point_two, w5u, w5s, w6u,
    )
    back = lax.all_to_all(
        rows.reshape(16, 4, 16, 128), PLANE, 0, 0, tiled=True, axis_index_groups=GROUPS
    )
    return call(from_rows_kernel, shape(32, 4, 4, 256))(back)


def solution(mesh):
    in_specs = (P(None, "gx", "gy", "gz"), P(), P(), P(), P(), P(), P(), P(), P(), P(), P())
    out_specs = P(None, "gx", "gy", "gz")
    return jax.shard_map(forward, mesh=mesh, in_specs=in_specs, out_specs=out_specs, check_vma=False)
```
